128 devices in a mesh: col: 32 (over z, y_hi, x), row: 4 (over y_lo, core).
Axes of the slice: x: 4, y: 4 (y_hi: 2, y_lo: 2; y = y_hi * 2 + y_lo), z: 4, core: 2. Of those that a mesh axis runs over, the one named last changes fastest.
Arguments:
- diffs: float32 [32768, 8192], P(('col', 'row')), as said below
- pairing: int32 [64], replicated, may hold values from 0 to 63, each once
Outputs:
- rotated: float32 [32, 4, 256, 8192], P(None, 'row', None, 'col')
The draws below stay inside these ranges and needn't reach their ends.
Inputs may be any that keep to these rules, and one draw needn't show every extreme that they name: `pairing`: a permutation: every block index appears once. `diffs`: token rows with finite entries.
All inputs are finite; a program needn't handle non-finite values.
Results may differ from the reference program's by a relative error of at most 0.00025.
Values sent between devices are 32-bit elements; how exact they have to be, the bound alone decides.
No kernel may reach another device: no remote copies, remote signals or barrier semaphores. Data moves between devices by JAX's collectives and lax.ppermute only.
A program may use at most 128 MiB of HBM per device.

```python
import math
import jax
import jax.numpy as jnp
from jax import lax

BLOCK = 128
ROW_DEV = 256
JACOBI_STEPS = 2
INNER_STEPS = 2
N_BLOCKS = 64
COLS = 8192
ROWS = 32768
N_COL = 32
N_ROW = 4


factor_count = 8


def draw_diffs(key, part):
    keys = jax.random.split(key, 5)
    position = jnp.arange(ROWS, dtype=jnp.float32) / ROWS
    noise = jax.random.normal(keys[0], (ROWS, COLS), jnp.float32)
    col_scale = jnp.exp(jax.random.uniform(keys[1], (COLS,), jnp.float32, 0.0, math.log(2.5)))
    row_scale = jnp.exp(math.log(3.0) * position + jax.random.uniform(keys[2], (ROWS,), jnp.float32, -0.3, 0.3))
    centers = (jnp.arange(factor_count, dtype=jnp.float32) + 0.5) / factor_count
    bumps = jnp.exp(-((position[:, None] - centers[None, :]) * factor_count) ** 2)
    loads = 0.2 * bumps * jax.random.normal(keys[3], (ROWS, factor_count), jnp.float32)
    mixing = jax.random.normal(keys[4], (factor_count, COLS), jnp.float32)
    shared = loads[:, 0:1] * mixing[0][None, :]
    for factor_index in range(1, factor_count):
        shared = shared + loads[:, factor_index:factor_index + 1] * mixing[factor_index][None, :]
    return (row_scale[:, None] * col_scale[None, :] * (noise + shared)).astype(jnp.float32)


def setup_inputs(seed: int = 0) -> dict:
    key_list = jax.random.split(jax.random.key(seed), 3)
    return {
        "diffs": draw_diffs(jax.random.fold_in(key_list[2], 71), 0),
        "pairing": jax.random.permutation(key_list[1], N_BLOCKS).astype(jnp.int32),
    }


def pair_rotation(pair_gram):
    rotation = jnp.eye(pair_gram.shape[0], dtype=jnp.float32)
    for repeat_index in range(INNER_STEPS):
        product = jnp.dot(pair_gram.astype(jnp.float32), rotation.astype(jnp.float32), precision=lax.Precision.HIGHEST, preferred_element_type=jnp.float32)
        normal_matrix = lax.dot_general(product.astype(jnp.float32), product.astype(jnp.float32), (((0,), (0,)), ((), ())), precision=lax.Precision.HIGHEST, preferred_element_type=jnp.float32)
        factor = jnp.linalg.cholesky(normal_matrix)
        rotation = lax.linalg.triangular_solve(factor, product.T, left_side=True, lower=True).T
    return rotation

def turn_pair(pair_rows):
    pair_gram = lax.dot_general(pair_rows.astype(jnp.float32), pair_rows.astype(jnp.float32), (((0,), (0,)), ((), ())), precision=lax.Precision.HIGHEST, preferred_element_type=jnp.float32)
    rotation = pair_rotation(pair_gram)
    return jnp.dot(pair_rows.astype(jnp.float32), rotation.astype(jnp.float32), precision=lax.Precision.HIGHEST, preferred_element_type=jnp.float32)

def move_blocks(pairs):
    upper_half = pairs[:, :, :BLOCK]
    lower_half = pairs[:, :, BLOCK:]
    new_upper = jnp.concatenate([upper_half[:1], lower_half[:1], upper_half[1:-1]], axis=0)
    new_lower = jnp.concatenate([lower_half[1:], upper_half[-1:]], axis=0)
    return jnp.concatenate([new_upper, new_lower], axis=2)

def reference(diffs, pairing):
    blocks = diffs.reshape(ROWS, N_BLOCKS, BLOCK)
    ordered = jnp.take(blocks, pairing.astype(jnp.int32), axis=1)
    pairs = jnp.transpose(ordered.reshape(ROWS, N_COL, 2 * BLOCK), (1, 0, 2))
    for jacobi_step in range(JACOBI_STEPS):
        if jacobi_step > 0:
            pairs = move_blocks(pairs)
        pairs = lax.map(turn_pair, pairs)
    final = jnp.transpose(pairs, (1, 0, 2)).reshape(ROWS, COLS)
    return final.reshape(N_COL, N_ROW, ROW_DEV, COLS)
```

```python
import functools

import jax
import jax.numpy as jnp
from jax import lax
from jax.experimental import pallas as pl
from jax.experimental.pallas import tpu as pltpu
from jax.sharding import PartitionSpec as P

BLOCK = 128
WIDTH = 2 * BLOCK
TILE = 1024
PANEL = 32
HIGHEST = lax.Precision.HIGHEST
COLUMNS = (((0,), (0,)), ((), ()))
LANES = (((1,), (1,)), ((), ()))
F32 = jnp.float32
BF16 = jnp.bfloat16


def grant(megabytes):
    return pltpu.CompilerParams(vmem_limit_bytes=megabytes << 20)


def two_terms(value):
    high = value.astype(BF16)
    return high, (value - high.astype(F32)).astype(BF16)


def three_terms(value):
    high = value.astype(BF16)
    rest = value - high.astype(F32)
    middle = rest.astype(BF16)
    return high, middle, (rest - middle.astype(F32)).astype(BF16)


def order_kernel(pairing_ref, first_ref, second_ref, out_ref):
    out_ref[0, :, :BLOCK] = first_ref[...]
    out_ref[0, :, BLOCK:] = second_ref[...]


def order_pairs(diffs, pairing):
    rows, columns = diffs.shape
    count = columns // WIDTH
    return pl.pallas_call(
        order_kernel,
        grid_spec=pltpu.PrefetchScalarGridSpec(
            num_scalar_prefetch=1,
            grid=(count,),
            in_specs=[
                pl.BlockSpec((rows, BLOCK), lambda p, pairing: (0, pairing[2 * p])),
                pl.BlockSpec((rows, BLOCK), lambda p, pairing: (0, pairing[2 * p + 1])),
            ],
            out_specs=pl.BlockSpec((1, rows, WIDTH), lambda p, pairing: (p, 0, 0)),
        ),
        out_shape=jax.ShapeDtypeStruct((count, rows, WIDTH), F32),
        compiler_params=grant(16),
        name="order",
    )(pairing, diffs, diffs)


def add_gram(tile, total_ref, cross_ref):
    high, low = two_terms(tile)
    total_ref[...] += lax.dot_general(high, high, COLUMNS, preferred_element_type=F32)
    cross_ref[...] += lax.dot_general(high, low, COLUMNS, preferred_element_type=F32)


def gram_kernel(tile_ref, total_ref, cross_ref):
    @pl.when(pl.program_id(0) == 0)
    def _():
        total_ref[...] = jnp.zeros_like(total_ref)
        cross_ref[...] = jnp.zeros_like(cross_ref)

    add_gram(tile_ref[...], total_ref, cross_ref)

    @pl.when(pl.program_id(0) == pl.num_programs(0) - 1)
    def _():
        total_ref[...] += cross_ref[...] + cross_ref[...].T


def local_gram(pair_rows):
    rows = pair_rows.shape[0]
    return pl.pallas_call(
        gram_kernel,
        grid=(rows // TILE,),
        in_specs=[pl.BlockSpec((TILE, WIDTH), lambda i: (i, 0))],
        out_specs=pl.BlockSpec((WIDTH, WIDTH), lambda i: (0, 0)),
        out_shape=jax.ShapeDtypeStruct((WIDTH, WIDTH), F32),
        scratch_shapes=[pltpu.VMEM((WIDTH, WIDTH), F32)],
        compiler_params=grant(16),
        name="gram",
    )(pair_rows)


def moved_tile(ends, from_below, kept_second, from_above, kept_first):
    upper = jnp.where(ends[0] == 1, kept_second, from_below)
    lower = jnp.where(ends[1] == 1, kept_first, from_above)
    return jnp.concatenate([upper, lower], axis=1)


def moved_gram_kernel(ends, below_ref, second_ref, above_ref, first_ref, total_ref, cross_ref):
    @pl.when(pl.program_id(0) == 0)
    def _():
        total_ref[...] = jnp.zeros_like(total_ref)
        cross_ref[...] = jnp.zeros_like(cross_ref)

    tile = moved_tile(ends, below_ref[...], second_ref[...], above_ref[...], first_ref[...])
    add_gram(tile, total_ref, cross_ref)

    @pl.when(pl.program_id(0) == pl.num_programs(0) - 1)
    def _():
        total_ref[...] += cross_ref[...] + cross_ref[...].T


def moved_specs():
    return [
        pl.BlockSpec((TILE, BLOCK), lambda i, ends: (i, 0)),
        pl.BlockSpec((TILE, BLOCK), lambda i, ends: (i * ends[0], 0)),
        pl.BlockSpec((TILE, BLOCK), lambda i, ends: (i, 0)),
        pl.BlockSpec((TILE, BLOCK), lambda i, ends: (i * ends[1], 0)),
    ]


def moved_gram(ends, moved):
    rows = moved[0].shape[0]
    return pl.pallas_call(
        moved_gram_kernel,
        grid_spec=pltpu.PrefetchScalarGridSpec(
            num_scalar_prefetch=1,
            grid=(rows // TILE,),
            in_specs=moved_specs(),
            out_specs=pl.BlockSpec((WIDTH, WIDTH), lambda i, ends: (0, 0)),
            scratch_shapes=[pltpu.VMEM((WIDTH, WIDTH), F32)],
        ),
        out_shape=jax.ShapeDtypeStruct((WIDTH, WIDTH), F32),
        compiler_params=grant(24),
        name="moved_gram",
    )(ends, *moved)


def row_total(partial_gram):
    count = lax.axis_size("row")
    step = 1
    while step < count:
        swap = [(source, source ^ step) for source in range(count)]
        partial_gram = partial_gram + lax.ppermute(partial_gram, "row", swap)
        step *= 2
    return partial_gram


def outer_product(left, right):
    left1, left2, left3 = three_terms(left)
    right1, right2, right3 = three_terms(right)
    left = jnp.concatenate([left1, left1, left2, left2, left1, left3], axis=0)
    right = jnp.concatenate([right1, right2, right1, right2, right3, right1], axis=0)
    return lax.dot_general(left, right, COLUMNS, preferred_element_type=F32)


def eliminate(work_ref, factor_ref, width):
    for start in range(0, WIDTH, PANEL):
        end = start + PANEL
        rows = work_ref[start:end, :width]
        row_id = lax.broadcasted_iota(jnp.int32, (PANEL, 1), 0)
        pivots = jnp.zeros((PANEL, 1), F32)
        for j in range(PANEL):
            column = rows[:, start + j : start + j + 1]
            pivot = column[j : j + 1, :]
            multiple = jnp.where(row_id > j, column / pivot, 0.0)
            pivots = jnp.where(row_id == j, pivot, pivots)
            rows = rows - multiple * rows[j : j + 1, :]
        rows = rows * lax.rsqrt(pivots)
        row_at = lax.broadcasted_iota(jnp.int32, (PANEL, width), 0) + start
        rows = jnp.where(lax.broadcasted_iota(jnp.int32, (PANEL, width), 1) >= row_at, rows, 0.0)
        factor_ref[start:end, :width] = rows
        if end < WIDTH:
            work_ref[end:, :width] -= outer_product(rows[:, end:WIDTH], rows)


def rotation_kernel(gram_ref, out_ref, work_ref, factor_ref):
    gram = gram_ref[...]
    work_ref[:, :WIDTH] = jnp.dot(gram, gram, precision=HIGHEST, preferred_element_type=F32)
    eliminate(work_ref, factor_ref, WIDTH)
    factor = factor_ref[:, :WIDTH]
    work_ref[:, :WIDTH] = lax.dot_general(
        factor, factor, LANES, precision=HIGHEST, preferred_element_type=F32
    )
    work_ref[:, WIDTH:] = factor
    eliminate(work_ref, factor_ref, 2 * WIDTH)
    out_ref[...] = factor_ref[:, WIDTH:]


def pair_rotation(pair_gram):
    return pl.pallas_call(
        rotation_kernel,
        out_shape=jax.ShapeDtypeStruct((WIDTH, WIDTH), F32),
        scratch_shapes=[pltpu.VMEM((WIDTH, 2 * WIDTH), F32)] * 2,
        compiler_params=grant(32),
        name="rotation",
    )(pair_gram)


def product(rows, rotation_t):
    high, low = two_terms(rows)
    turn_high, turn_low = two_terms(rotation_t)
    turned = lax.dot_general(high, turn_high, LANES, preferred_element_type=F32)
    turned += lax.dot_general(low, turn_high, LANES, preferred_element_type=F32)
    return turned + lax.dot_general(high, turn_low, LANES, preferred_element_type=F32)


def turn_kernel(rows_ref, rotation_ref, first_ref, second_ref):
    turned = product(rows_ref[...], rotation_ref[...])
    first_ref[...] = turned[:, :BLOCK]
    second_ref[...] = turned[:, BLOCK:]


def turn(pair_rows, rotation_t):
    rows = pair_rows.shape[0]
    half = pl.BlockSpec((TILE, BLOCK), lambda i: (i, 0))
    return pl.pallas_call(
        turn_kernel,
        grid=(rows // TILE,),
        in_specs=[
            pl.BlockSpec((TILE, WIDTH), lambda i: (i, 0)),
            pl.BlockSpec((WIDTH, WIDTH), lambda i: (0, 0)),
        ],
        out_specs=[half, half],
        out_shape=[jax.ShapeDtypeStruct((rows, BLOCK), F32)] * 2,
        compiler_params=grant(24),
        name="turn",
    )(pair_rows, rotation_t)


def moved_turn_kernel(ends, below_ref, second_ref, above_ref, first_ref, rotation_ref, out_ref):
    tile = moved_tile(ends, below_ref[...], second_ref[...], above_ref[...], first_ref[...])
    out_ref[...] = product(tile, rotation_ref[...])


def moved_turn(ends, moved, rotation_t):
    rows = moved[0].shape[0]
    return pl.pallas_call(
        moved_turn_kernel,
        grid_spec=pltpu.PrefetchScalarGridSpec(
            num_scalar_prefetch=1,
            grid=(rows // TILE,),
            in_specs=moved_specs() + [pl.BlockSpec((WIDTH, WIDTH), lambda i, ends: (0, 0))],
            out_specs=pl.BlockSpec((TILE, WIDTH), lambda i, ends: (i, 0)),
        ),
        out_shape=jax.ShapeDtypeStruct((rows, WIDTH), F32),
        compiler_params=grant(24),
        name="moved_turn",
    )(ends, *moved, rotation_t)


def local(diffs, pairing):
    col_count = lax.axis_size("col")
    position = lax.axis_index("col")
    local_rows = diffs.shape[0]
    ends = jnp.stack([position == 0, position == col_count - 1]).astype(jnp.int32)
    ordered = order_pairs(diffs, pairing)
    pair_rows = lax.all_to_all(ordered, "col", split_axis=0, concat_axis=0, tiled=True)
    pair_rows = pair_rows.reshape(-1, WIDTH)

    rotation_t = pair_rotation(row_total(local_gram(pair_rows)))
    swapped = jnp.concatenate([rotation_t[BLOCK:], rotation_t[:BLOCK]])
    first, second = turn(pair_rows, jnp.where(position == 0, swapped, rotation_t))
    above = lax.ppermute(second, "col", [(p, p - 1) for p in range(1, col_count)])
    below = lax.ppermute(first, "col", [(p, p + 1) for p in range(col_count - 1)])

    moved = (below, second, above, first)
    rotation_t = pair_rotation(row_total(moved_gram(ends, moved)))
    return moved_turn(ends, moved, rotation_t).reshape(col_count, 1, local_rows, WIDTH)


def solution(mesh):
    in_specs = (P(("col", "row"), None), P())
    out_specs = P(None, "row", None, "col")
    return jax.shard_map(local, mesh=mesh, in_specs=in_specs, out_specs=out_specs, check_vma=False)
```

```python
import functools

import jax
import jax.numpy as jnp
from jax import lax
from jax.experimental import pallas as pl
from jax.experimental.pallas import tpu as pltpu
from jax.sharding import PartitionSpec as P

BLOCK = 128
WIDTH = 2 * BLOCK
TILE = 1024
PANEL = 32
SUB = 8
HIGHEST = lax.Precision.HIGHEST
COLUMNS = (((0,), (0,)), ((), ()))
LANES = (((1,), (1,)), ((), ()))
F32 = jnp.float32
BF16 = jnp.bfloat16


def grant(megabytes):
    return pltpu.CompilerParams(vmem_limit_bytes=megabytes << 20)


def two_terms(value):
    high = value.astype(BF16)
    return high, (value - high.astype(F32)).astype(BF16)


def three_terms(value):
    high = value.astype(BF16)
    rest = value - high.astype(F32)
    middle = rest.astype(BF16)
    return high, middle, (rest - middle.astype(F32)).astype(BF16)


def order_kernel(pairing_ref, diffs_ref, out_ref, sems):
    count = pairing_ref.shape[0]

    def copy(block):
        column = pl.multiple_of(pairing_ref[block] * BLOCK, BLOCK)
        half = pl.ds((block % 2) * BLOCK, BLOCK)
        return pltpu.make_async_copy(
            diffs_ref.at[:, pl.ds(column, BLOCK)],
            out_ref.at[block // 2, :, half],
            sems.at[block],
        )

    for block in range(count):
        copy(block).start()
    for block in range(count):
        copy(block).wait()


def order_pairs(diffs, pairing):
    rows, columns = diffs.shape
    return pl.pallas_call(
        order_kernel,
        in_specs=[
            pl.BlockSpec(memory_space=pltpu.SMEM),
            pl.BlockSpec(memory_space=pltpu.HBM),
        ],
        out_specs=pl.BlockSpec(memory_space=pl.ANY),
        out_shape=jax.ShapeDtypeStruct((columns // WIDTH, rows, WIDTH), F32),
        scratch_shapes=[pltpu.SemaphoreType.DMA((columns // BLOCK,))],
        compiler_params=grant(2),
        name="order",
    )(pairing, diffs)


def add_gram(tile, total_ref, cross_ref):
    high, low = two_terms(tile)
    total_ref[...] += lax.dot_general(high, high, COLUMNS, preferred_element_type=F32)
    cross_ref[...] += lax.dot_general(high, low, COLUMNS, preferred_element_type=F32)


def gram_kernel(tile_ref, total_ref, cross_ref):
    @pl.when(pl.program_id(0) == 0)
    def _():
        total_ref[...] = jnp.zeros_like(total_ref)
        cross_ref[...] = jnp.zeros_like(cross_ref)

    add_gram(tile_ref[...], total_ref, cross_ref)

    @pl.when(pl.program_id(0) == pl.num_programs(0) - 1)
    def _():
        total_ref[...] += cross_ref[...] + cross_ref[...].T


def local_gram(pair_rows):
    rows = pair_rows.shape[0]
    return pl.pallas_call(
        gram_kernel,
        grid=(rows // TILE,),
        in_specs=[pl.BlockSpec((TILE, WIDTH), lambda i: (i, 0))],
        out_specs=pl.BlockSpec((WIDTH, WIDTH), lambda i: (0, 0)),
        out_shape=jax.ShapeDtypeStruct((WIDTH, WIDTH), F32),
        scratch_shapes=[pltpu.VMEM((WIDTH, WIDTH), F32)],
        compiler_params=grant(8),
        name="gram",
    )(pair_rows)


def moved_tile(ends, from_below, kept_second, from_above, kept_first):
    upper = jnp.where(ends[0] == 1, kept_second, from_below)
    lower = jnp.where(ends[1] == 1, kept_first, from_above)
    return jnp.concatenate([upper, lower], axis=1)


def moved_gram_kernel(ends, below_ref, second_ref, above_ref, first_ref, total_ref, cross_ref):
    @pl.when(pl.program_id(0) == 0)
    def _():
        total_ref[...] = jnp.zeros_like(total_ref)
        cross_ref[...] = jnp.zeros_like(cross_ref)

    tile = moved_tile(ends, below_ref[...], second_ref[...], above_ref[...], first_ref[...])
    add_gram(tile, total_ref, cross_ref)

    @pl.when(pl.program_id(0) == pl.num_programs(0) - 1)
    def _():
        total_ref[...] += cross_ref[...] + cross_ref[...].T


def moved_specs():
    return [
        pl.BlockSpec((TILE, BLOCK), lambda i, ends: (i, 0)),
        pl.BlockSpec((TILE, BLOCK), lambda i, ends: (i * ends[0], 0)),
        pl.BlockSpec((TILE, BLOCK), lambda i, ends: (i, 0)),
        pl.BlockSpec((TILE, BLOCK), lambda i, ends: (i * ends[1], 0)),
    ]


def moved_gram(ends, moved):
    rows = moved[0].shape[0]
    return pl.pallas_call(
        moved_gram_kernel,
        grid_spec=pltpu.PrefetchScalarGridSpec(
            num_scalar_prefetch=1,
            grid=(rows // TILE,),
            in_specs=moved_specs(),
            out_specs=pl.BlockSpec((WIDTH, WIDTH), lambda i, ends: (0, 0)),
            scratch_shapes=[pltpu.VMEM((WIDTH, WIDTH), F32)],
        ),
        out_shape=jax.ShapeDtypeStruct((WIDTH, WIDTH), F32),
        compiler_params=grant(12),
        name="moved_gram",
    )(ends, *moved)


def row_total(partial_gram):
    count = lax.axis_size("row")
    step = 1
    while step < count:
        swap = [(source, source ^ step) for source in range(count)]
        partial_gram = partial_gram + lax.ppermute(partial_gram, "row", swap)
        step *= 2
    return partial_gram


def outer_product(left, right):
    left1, left2, left3 = three_terms(left)
    right1, right2, right3 = three_terms(right)
    left = jnp.concatenate([left1, left1, left2, left2, left1, left3], axis=0)
    right = jnp.concatenate([right1, right2, right1, right2, right3, right1], axis=0)
    return lax.dot_general(left, right, COLUMNS, preferred_element_type=F32)


def spread(value):
    return jnp.broadcast_to(value, (SUB, BLOCK))


def total(terms):
    while len(terms) > 1:
        paired = [a + b for a, b in zip(terms[::2], terms[1::2])]
        terms = paired + terms[len(terms) - len(terms) % 2 :]
    return terms[0]


def small_inverse(tile, lane, spread_ref, base):
    for j in range(SUB):
        spread_ref[base + SUB * j : base + SUB * (j + 1), :] = spread(tile[:, lane + j : lane + j + 1])
    entry = {
        (i, j): spread_ref[pl.ds(base + SUB * j + i, SUB, stride=0), :]
        for j in range(SUB)
        for i in range(j, SUB)
    }
    lower, scales = {}, []
    for j in range(SUB):
        scale = lax.rsqrt(entry[j, j])
        inverse = scale * scale
        scales.append(scale)
        for i in range(j + 1, SUB):
            lower[i, j] = entry[i, j] * inverse
        for m in range(j + 1, SUB):
            for i in range(m, SUB):
                entry[i, m] = entry[i, m] - lower[i, j] * entry[m, j]
    solved = {}
    for j in range(SUB):
        for i in range(j + 1, SUB):
            terms = [lower[i, j]] + [lower[i, m] * solved[m, j] for m in range(j + 1, i)]
            solved[i, j] = -total(terms)
    solved = {at: value * scales[at[0]] for at, value in solved.items()}
    return solved | {(j, j): scales[j] for j in range(SUB)}


def tiles_of(ref, start, end, first, last):
    return jnp.concatenate([ref[t, start:end, :] for t in range(first, last)], axis=1)


def put_tiles(ref, first, value):
    for t in range(value.shape[1] // BLOCK):
        ref[first + t] = value[:, BLOCK * t : BLOCK * (t + 1)]


def eliminate(work_ref, factor_ref, spread_ref, tiles):
    row = lax.broadcasted_iota(jnp.int32, (SUB, BLOCK), 0)
    lane = lax.broadcasted_iota(jnp.int32, (SUB, BLOCK), 1)
    zero = jnp.zeros((SUB, BLOCK), F32)
    for start in range(0, WIDTH, PANEL):
        end = start + PANEL
        own = start // BLOCK
        for top in range(start, end, SUB):
            at = top % BLOCK
            base = SUB * SUB * (top // SUB % 2)
            small = small_inverse(work_ref[own, top : top + SUB, :], at, spread_ref, base)
            columns = []
            for j in range(SUB):
                column = zero
                for i in range(j, SUB):
                    column = jnp.where(row == i, small[i, j], column)
                columns.append(column)
            for t in range(tiles):
                if t < own:
                    solved = zero
                else:
                    solved = total(
                        [columns[j] * work_ref[t, pl.ds(top + j, SUB, stride=0), :] for j in range(SUB)]
                    )
                    if t == own:
                        solved = jnp.where(lane >= row + at, solved, 0.0)
                factor_ref[t, top : top + SUB, :] = solved
            for below in range(top + SUB, end, SUB):
                tile = work_ref[own, below : below + SUB, :]
                entries = [spread(tile[:, at + j : at + j + 1]) for j in range(SUB)]
                left = [total([entries[j] * small[i, j] for j in range(i + 1)]) for i in range(SUB)]
                for t in range(own, tiles):
                    work_ref[t, below : below + SUB, :] -= total(
                        [left[i] * factor_ref[t, pl.ds(top + i, SUB, stride=0), :] for i in range(SUB)]
                    )
        if end < WIDTH:
            first = end // BLOCK
            update = outer_product(
                tiles_of(factor_ref, start, end, first, WIDTH // BLOCK),
                tiles_of(factor_ref, start, end, first, tiles),
            )
            for t in range(first, tiles):
                here = BLOCK * (t - first)
                work_ref[t, end:, :] -= update[end - BLOCK * first :, here : here + BLOCK]


def rotation_kernel(gram_ref, out_ref, work_ref, factor_ref, spread_ref):
    gram = gram_ref[...]
    square = jnp.dot(gram, gram, precision=HIGHEST, preferred_element_type=F32)
    put_tiles(work_ref, 0, square)
    eliminate(work_ref, factor_ref, spread_ref, WIDTH // BLOCK)
    factor = tiles_of(factor_ref, 0, WIDTH, 0, WIDTH // BLOCK)
    square = lax.dot_general(factor, factor, LANES, precision=HIGHEST, preferred_element_type=F32)
    put_tiles(work_ref, 0, square)
    put_tiles(work_ref, WIDTH // BLOCK, factor)
    eliminate(work_ref, factor_ref, spread_ref, 2 * WIDTH // BLOCK)
    out_ref[...] = tiles_of(factor_ref, 0, WIDTH, WIDTH // BLOCK, 2 * WIDTH // BLOCK)


def pair_rotation(pair_gram):
    tiles = pltpu.VMEM((2 * WIDTH // BLOCK, WIDTH, BLOCK), F32)
    return pl.pallas_call(
        rotation_kernel,
        out_shape=jax.ShapeDtypeStruct((WIDTH, WIDTH), F32),
        scratch_shapes=[tiles, tiles, pltpu.VMEM((2 * SUB * SUB, BLOCK), F32)],
        compiler_params=grant(8),
        cost_estimate=pl.CostEstimate(flops=20_000_000_000, bytes_accessed=1 << 19, transcendentals=0),
        name="rotation",
    )(pair_gram)


def product(rows, rotation_t):
    high, low = two_terms(rows)
    turn_high, turn_low = two_terms(rotation_t)
    turned = lax.dot_general(high, turn_high, LANES, preferred_element_type=F32)
    turned += lax.dot_general(low, turn_high, LANES, preferred_element_type=F32)
    return turned + lax.dot_general(high, turn_low, LANES, preferred_element_type=F32)


def turn_kernel(rows_ref, rotation_ref, first_ref, second_ref):
    turned = product(rows_ref[...], rotation_ref[...])
    first_ref[...] = turned[:, :BLOCK]
    second_ref[...] = turned[:, BLOCK:]


def turn(pair_rows, rotation_t):
    rows = pair_rows.shape[0]
    half = pl.BlockSpec((TILE, BLOCK), lambda i: (i, 0))
    return pl.pallas_call(
        turn_kernel,
        grid=(rows // TILE,),
        in_specs=[
            pl.BlockSpec((TILE, WIDTH), lambda i: (i, 0)),
            pl.BlockSpec((WIDTH, WIDTH), lambda i: (0, 0)),
        ],
        out_specs=[half, half],
        out_shape=[jax.ShapeDtypeStruct((rows, BLOCK), F32)] * 2,
        compiler_params=grant(12),
        name="turn",
    )(pair_rows, rotation_t)


def moved_turn_kernel(ends, below_ref, second_ref, above_ref, first_ref, rotation_ref, out_ref):
    tile = moved_tile(ends, below_ref[...], second_ref[...], above_ref[...], first_ref[...])
    out_ref[...] = product(tile, rotation_ref[...])


def moved_turn(ends, moved, rotation_t):
    rows = moved[0].shape[0]
    return pl.pallas_call(
        moved_turn_kernel,
        grid_spec=pltpu.PrefetchScalarGridSpec(
            num_scalar_prefetch=1,
            grid=(rows // TILE,),
            in_specs=moved_specs() + [pl.BlockSpec((WIDTH, WIDTH), lambda i, ends: (0, 0))],
            out_specs=pl.BlockSpec((TILE, WIDTH), lambda i, ends: (i, 0)),
        ),
        out_shape=jax.ShapeDtypeStruct((rows, WIDTH), F32),
        compiler_params=grant(12),
        name="moved_turn",
    )(ends, *moved, rotation_t)


def local(diffs, pairing):
    col_count = lax.axis_size("col")
    position = lax.axis_index("col")
    local_rows = diffs.shape[0]
    ends = jnp.stack([position == 0, position == col_count - 1]).astype(jnp.int32)
    ordered = order_pairs(diffs, pairing)
    pair_rows = lax.all_to_all(ordered, "col", split_axis=0, concat_axis=0, tiled=True)
    pair_rows = pair_rows.reshape(-1, WIDTH)

    rotation_t = pair_rotation(row_total(local_gram(pair_rows)))
    swapped = jnp.concatenate([rotation_t[BLOCK:], rotation_t[:BLOCK]])
    first, second = turn(pair_rows, jnp.where(position == 0, swapped, rotation_t))
    above = lax.ppermute(second, "col", [(p, p - 1) for p in range(1, col_count)])
    below = lax.ppermute(first, "col", [(p, p + 1) for p in range(col_count - 1)])

    moved = (below, second, above, first)
    rotation_t = pair_rotation(row_total(moved_gram(ends, moved)))
    return moved_turn(ends, moved, rotation_t).reshape(col_count, 1, local_rows, WIDTH)


def solution(mesh):
    in_specs = (P(("col", "row"), None), P())
    out_specs = P(None, "row", None, "col")
    return jax.shard_map(local, mesh=mesh, in_specs=in_specs, out_specs=out_specs, check_vma=False)
```

```python
import functools

import jax
import jax.numpy as jnp
from jax import lax
from jax.experimental import pallas as pl
from jax.experimental.pallas import tpu as pltpu
from jax.sharding import PartitionSpec as P

BLOCK = 128
WIDTH = 2 * BLOCK
TILE = 512
RAW = 2 * TILE
MAIN = 10 * TILE
PANEL = 32
SUB = 8
HIGHEST = lax.Precision.HIGHEST
COLUMNS = (((0,), (0,)), ((), ()))
LANES = (((1,), (1,)), ((), ()))
F32 = jnp.float32
BF16 = jnp.bfloat16


def grant(megabytes):
    return pltpu.CompilerParams(vmem_limit_bytes=megabytes << 20)


def in_hbm(value):
    return pltpu.with_memory_space_constraint(value, pltpu.HBM)


def two_terms(value):
    high = value.astype(BF16)
    return high, (value - high.astype(F32)).astype(BF16)


def three_terms(value):
    high = value.astype(BF16)
    rest = value - high.astype(F32)
    middle = rest.astype(BF16)
    return high, middle, (rest - middle.astype(F32)).astype(BF16)


def order_kernel(pairing_ref, diffs_ref, out_ref, sems):
    count = pairing_ref.shape[0]

    def copy(block):
        column = pl.multiple_of(pairing_ref[block] * BLOCK, BLOCK)
        half = pl.ds((block % 2) * BLOCK, BLOCK)
        return pltpu.make_async_copy(
            diffs_ref.at[:, pl.ds(column, BLOCK)],
            out_ref.at[block // 2, :, half],
            sems.at[block],
        )

    for block in range(count):
        copy(block).start()
    for block in range(count):
        copy(block).wait()


def order_pairs(diffs, pairing):
    rows, columns = diffs.shape
    return pl.pallas_call(
        order_kernel,
        in_specs=[
            pl.BlockSpec(memory_space=pltpu.SMEM),
            pl.BlockSpec(memory_space=pl.ANY),
        ],
        out_specs=pl.BlockSpec(memory_space=pl.ANY),
        out_shape=jax.ShapeDtypeStruct((columns // WIDTH, rows, WIDTH), F32),
        scratch_shapes=[pltpu.SemaphoreType.DMA((columns // BLOCK,))],
        compiler_params=grant(2),
        name="order",
    )(pairing, diffs)


def add_gram(tile, total_ref, cross_ref):
    high, low = two_terms(tile)
    total_ref[...] += lax.dot_general(high, high, COLUMNS, preferred_element_type=F32)
    cross_ref[...] += lax.dot_general(high, low, COLUMNS, preferred_element_type=F32)


def row_copy(source_ref, rows_ref, sems, tile, first=0):
    source = source_ref.at[pl.ds(pl.multiple_of((tile + first) * TILE, TILE), TILE), :]
    rows = rows_ref.at[pl.ds(pl.multiple_of(tile * TILE, TILE), TILE), :]
    return pltpu.make_async_copy(source, rows, sems.at[tile])


def pack(total_ref, cross_ref):
    gram = total_ref[...] + (cross_ref[...] + cross_ref[...].T)
    return jnp.concatenate([gram[:BLOCK, :BLOCK], gram[:BLOCK, BLOCK:], gram[BLOCK:, BLOCK:]])


def unpack(packed):
    corner, side, end = packed[:BLOCK], packed[BLOCK : 2 * BLOCK], packed[2 * BLOCK :]
    upper = jnp.concatenate([corner, side], axis=1)
    return jnp.concatenate([upper, jnp.concatenate([side.T, end], axis=1)])


def gram_kernel(source_ref, out_ref, total_ref, cross_ref, rows_ref, sems):
    tiles = rows_ref.shape[0] // TILE
    for tile in range(tiles):
        row_copy(source_ref, rows_ref, sems, tile).start()
    total_ref[...] = jnp.zeros_like(total_ref)
    cross_ref[...] = jnp.zeros_like(cross_ref)

    @pl.loop(0, tiles)
    def _(tile):
        row_copy(source_ref, rows_ref, sems, tile).wait()
        rows = rows_ref[pl.ds(pl.multiple_of(tile * TILE, TILE), TILE), :]
        add_gram(rows, total_ref, cross_ref)

    out_ref[...] = pack(total_ref, cross_ref)


def local_gram(pair_rows):
    rows = pair_rows.shape[0]
    whole = pl.BlockSpec(memory_space=pltpu.VMEM)
    return pl.pallas_call(
        gram_kernel,
        in_specs=[pl.BlockSpec(memory_space=pltpu.HBM)],
        out_specs=whole,
        out_shape=jax.ShapeDtypeStruct((3 * BLOCK, BLOCK), F32),
        scratch_shapes=[
            pltpu.VMEM((WIDTH, WIDTH), F32),
            pltpu.VMEM((WIDTH, WIDTH), F32),
            pltpu.VMEM((rows, WIDTH), F32),
            pltpu.SemaphoreType.DMA((rows // TILE,)),
        ],
        compiler_params=grant(14),
        cost_estimate=pl.CostEstimate(flops=1000, bytes_accessed=1000, transcendentals=0),
        name="gram",
    )(in_hbm(pair_rows))


def cost(rows):
    return pl.CostEstimate(
        flops=6 * rows * WIDTH * WIDTH, bytes_accessed=8 * rows * WIDTH, transcendentals=0
    )


def half_copies(source_ref, rows_ref, sems, tile, first, column):
    rows = pl.ds(pl.multiple_of(tile * TILE, TILE), TILE)
    source = source_ref.at[pl.ds(pl.multiple_of((tile - first) * TILE, TILE), TILE), :]
    half = pl.ds(column * BLOCK, BLOCK)
    return pltpu.make_async_copy(source, rows_ref.at[rows, half], sems.at[column, tile])


def start_moved(ends, moved_refs, rows_ref, sems, first):
    below_ref, second_ref, above_ref, first_ref = moved_refs
    tiles = below_ref.shape[0] // TILE
    for column, arrived_ref, kept_ref in ((0, below_ref, second_ref), (1, above_ref, first_ref)):

        @pl.when(ends[column] == 1)
        def _():
            for tile in range(first, first + tiles):
                half_copies(kept_ref, rows_ref, sems, tile, first, column).start()

        @pl.when(ends[column] == 0)
        def _():
            for tile in range(first, first + tiles):
                half_copies(arrived_ref, rows_ref, sems, tile, first, column).start()


def wait_tile(like_ref, rows_ref, sems, tile):
    rows = pl.ds(pl.multiple_of(tile * TILE, TILE), TILE)
    for column in range(2):
        half = rows_ref.at[rows, pl.ds(column * BLOCK, BLOCK)]
        pltpu.make_async_copy(like_ref.at[pl.ds(0, TILE), :], half, sems.at[column, tile]).wait()
    return rows_ref[rows, :]


def moved_gram_kernel(ends, before_ref, *refs):
    moved_refs, (out_ref, total_ref, cross_ref, rows_ref, sems) = refs[:4], refs[4:]
    start_moved(ends, moved_refs, rows_ref, sems, 0)
    total_ref[...] = jnp.zeros_like(total_ref)
    cross_ref[...] = jnp.zeros_like(cross_ref)

    @pl.loop(0, rows_ref.shape[0] // TILE)
    def _(tile):
        add_gram(wait_tile(moved_refs[0], rows_ref, sems, tile), total_ref, cross_ref)

    out_ref[...] = before_ref[...] + pack(total_ref, cross_ref)


def moved_gram(ends, before, moved):
    rows = moved[0].shape[0]
    whole = pl.BlockSpec(memory_space=pltpu.VMEM)
    return pl.pallas_call(
        moved_gram_kernel,
        in_specs=[pl.BlockSpec(memory_space=pltpu.SMEM), whole] + [pl.BlockSpec(memory_space=pl.ANY)] * 4,
        out_specs=whole,
        out_shape=jax.ShapeDtypeStruct((3 * BLOCK, BLOCK), F32),
        scratch_shapes=[
            pltpu.VMEM((WIDTH, WIDTH), F32),
            pltpu.VMEM((WIDTH, WIDTH), F32),
            pltpu.VMEM((rows, WIDTH), F32),
            pltpu.SemaphoreType.DMA((2, rows // TILE)),
        ],
        compiler_params=grant(12),
        cost_estimate=cost(rows),
        name="moved_gram",
    )(ends, before, *moved)


def row_parts(packed):
    count = lax.axis_size("row")
    step = 1
    while True:
        swap = [(source, source ^ step) for source in range(count)]
        parts = (packed, lax.ppermute(packed, "row", swap))
        step *= 2
        if step >= count:
            return parts
        packed = parts[0] + parts[1]


def outer_product(left, right):
    left1, left2, left3 = three_terms(left)
    right1, right2, right3 = three_terms(right)
    left = jnp.concatenate([left1, left1, left2, left2, left1, left3], axis=0)
    right = jnp.concatenate([right1, right2, right1, right2, right3, right1], axis=0)
    return lax.dot_general(left, right, COLUMNS, preferred_element_type=F32)


def spread(value):
    return jnp.broadcast_to(value, (SUB, BLOCK))


def total(terms):
    while len(terms) > 1:
        paired = [a + b for a, b in zip(terms[::2], terms[1::2])]
        terms = paired + terms[len(terms) - len(terms) % 2 :]
    return terms[0]


def small_inverse(tile, lane, spread_ref, base):
    for j in range(SUB):
        spread_ref[base + SUB * j : base + SUB * (j + 1), :] = spread(tile[:, lane + j : lane + j + 1])
    entry = {
        (i, j): spread_ref[pl.ds(base + SUB * j + i, SUB, stride=0), :]
        for j in range(SUB)
        for i in range(j, SUB)
    }
    lower, scales = {}, []
    for j in range(SUB):
        scale = lax.rsqrt(entry[j, j])
        inverse = scale * scale
        scales.append(scale)
        for i in range(j + 1, SUB):
            lower[i, j] = entry[i, j] * inverse
        for m in range(j + 1, SUB):
            for i in range(m, SUB):
                entry[i, m] = entry[i, m] - lower[i, j] * entry[m, j]
    solved = {}
    for j in range(SUB):
        for i in range(j + 1, SUB):
            terms = [lower[i, j]] + [lower[i, m] * solved[m, j] for m in range(j + 1, i)]
            solved[i, j] = -total(terms)
    solved = {at: value * scales[at[0]] for at, value in solved.items()}
    return solved | {(j, j): scales[j] for j in range(SUB)}


def tiles_of(ref, start, end, first, last):
    return jnp.concatenate([ref[t, start:end, :] for t in range(first, last)], axis=1)


def put_tiles(ref, first, value):
    for t in range(value.shape[1] // BLOCK):
        ref[first + t] = value[:, BLOCK * t : BLOCK * (t + 1)]


def eliminate(work_ref, factor_ref, spread_ref, tiles):
    row = lax.broadcasted_iota(jnp.int32, (SUB, BLOCK), 0)
    lane = lax.broadcasted_iota(jnp.int32, (SUB, BLOCK), 1)
    zero = jnp.zeros((SUB, BLOCK), F32)
    for start in range(0, WIDTH, PANEL):
        end = start + PANEL
        own = start // BLOCK
        for top in range(start, end, SUB):
            at = top % BLOCK
            base = SUB * SUB * (top // SUB % 2)
            small = small_inverse(work_ref[own, top : top + SUB, :], at, spread_ref, base)
            columns = []
            for j in range(SUB):
                column = zero
                for i in range(j, SUB):
                    column = jnp.where(row == i, small[i, j], column)
                columns.append(column)
            for t in range(tiles):
                if t < own:
                    solved = zero
                else:
                    solved = total(
                        [columns[j] * work_ref[t, pl.ds(top + j, SUB, stride=0), :] for j in range(SUB)]
                    )
                    if t == own:
                        solved = jnp.where(lane >= row + at, solved, 0.0)
                factor_ref[t, top : top + SUB, :] = solved
            for below in range(top + SUB, end, SUB):
                tile = work_ref[own, below : below + SUB, :]
                entries = [spread(tile[:, at + j : at + j + 1]) for j in range(SUB)]
                left = [total([entries[j] * small[i, j] for j in range(i + 1)]) for i in range(SUB)]
                for t in range(own, tiles):
                    work_ref[t, below : below + SUB, :] -= total(
                        [left[i] * factor_ref[t, pl.ds(top + i, SUB, stride=0), :] for i in range(SUB)]
                    )
        if end < WIDTH:
            first = end // BLOCK
            update = outer_product(
                tiles_of(factor_ref, start, end, first, WIDTH // BLOCK),
                tiles_of(factor_ref, start, end, first, tiles),
            )
            for t in range(first, tiles):
                here = BLOCK * (t - first)
                work_ref[t, end:, :] -= update[end - BLOCK * first :, here : here + BLOCK]


def rotation_kernel(swap_ref, one_ref, two_ref, first_ref, second_ref, work_ref, factor_ref, spread_ref):
    gram = unpack(one_ref[...] + two_ref[...])
    square = jnp.dot(gram, gram, precision=HIGHEST, preferred_element_type=F32)
    put_tiles(work_ref, 0, square)
    eliminate(work_ref, factor_ref, spread_ref, WIDTH // BLOCK)
    factor = tiles_of(factor_ref, 0, WIDTH, 0, WIDTH // BLOCK)
    square = lax.dot_general(factor, factor, LANES, precision=HIGHEST, preferred_element_type=F32)
    put_tiles(work_ref, 0, square)
    put_tiles(work_ref, WIDTH // BLOCK, factor)
    eliminate(work_ref, factor_ref, spread_ref, 2 * WIDTH // BLOCK)
    halves = [
        tiles_of(factor_ref, start, start + BLOCK, WIDTH // BLOCK, 2 * WIDTH // BLOCK)
        for start in (0, BLOCK)
    ]
    first_ref[...] = jnp.where(swap_ref[0] == 1, halves[1], halves[0])
    second_ref[...] = jnp.where(swap_ref[0] == 1, halves[0], halves[1])


def pair_rotation(swap, parts):
    tiles = pltpu.VMEM((2 * WIDTH // BLOCK, WIDTH, BLOCK), F32)
    return pl.pallas_call(
        rotation_kernel,
        in_specs=[pl.BlockSpec(memory_space=pltpu.SMEM)] + [pl.BlockSpec(memory_space=pltpu.VMEM)] * 2,
        out_shape=[jax.ShapeDtypeStruct((BLOCK, WIDTH), F32)] * 2,
        scratch_shapes=[tiles, tiles, pltpu.VMEM((2 * SUB * SUB, BLOCK), F32)],
        compiler_params=grant(8),
        cost_estimate=pl.CostEstimate(flops=1000, bytes_accessed=1000, transcendentals=0),
        name="rotation",
    )(swap, *parts)


def product(rows, rotation_t):
    high, low = two_terms(rows)
    turn_high, turn_low = two_terms(rotation_t)
    turned = lax.dot_general(high, turn_high, LANES, preferred_element_type=F32)
    turned += lax.dot_general(low, turn_high, LANES, preferred_element_type=F32)
    return turned + lax.dot_general(high, turn_low, LANES, preferred_element_type=F32)


def turn_kernel(start, source_ref, one_ref, two_ref, first_ref, second_ref, rows_ref, sems):
    tiles = rows_ref.shape[0] // TILE
    for tile in range(tiles):
        row_copy(source_ref, rows_ref, sems, tile, start // TILE).start()
    rotation_t = jnp.concatenate([one_ref[...], two_ref[...]])

    @pl.loop(0, tiles)
    def _(tile):
        row_copy(source_ref, rows_ref, sems, tile, start // TILE).wait()
        rows = pl.ds(pl.multiple_of(tile * TILE, TILE), TILE)
        turned = product(rows_ref[rows, :], rotation_t)
        first_ref[rows, :] = turned[:, :BLOCK]
        second_ref[rows, :] = turned[:, BLOCK:]


def turn(pair_rows, rotation_t, start, end):
    rows = end - start
    whole = pl.BlockSpec(memory_space=pltpu.VMEM)
    return pl.pallas_call(
        functools.partial(turn_kernel, start),
        in_specs=[pl.BlockSpec(memory_space=pltpu.HBM), whole, whole],
        out_specs=[whole, whole],
        out_shape=[jax.ShapeDtypeStruct((rows, BLOCK), F32)] * 2,
        scratch_shapes=[
            pltpu.VMEM((rows, WIDTH), F32),
            pltpu.SemaphoreType.DMA((rows // TILE,)),
        ],
        compiler_params=grant(16),
        cost_estimate=cost(rows),
        name="turn",
    )(in_hbm(pair_rows), *rotation_t)


def raw_turn_kernel(ends, *refs):
    below_ref, above_ref, own_ref, first_ref, second_ref, below_t_ref, above_t_ref = refs[:7]
    out_ref, packed_ref, total_ref, cross_ref = refs[7:]

    @pl.when(pl.program_id(0) == 0)
    def _():
        total_ref[...] = jnp.zeros_like(total_ref)
        cross_ref[...] = jnp.zeros_like(cross_ref)

    own = own_ref[...]
    upper_t = jnp.where(ends[0] == 1, second_ref[...], below_t_ref[...])
    lower_t = jnp.where(ends[1] == 1, first_ref[...], above_t_ref[...])
    upper = product(jnp.where(ends[0] == 1, own, below_ref[...]), upper_t)
    lower = product(jnp.where(ends[1] == 1, own, above_ref[...]), lower_t)
    tile = jnp.concatenate([upper, lower], axis=1)
    out_ref[...] = tile
    add_gram(tile, total_ref, cross_ref)

    @pl.when(pl.program_id(0) == pl.num_programs(0) - 1)
    def _():
        packed_ref[...] = pack(total_ref, cross_ref)


def raw_turn(ends, below, above, own, *rotations_t):
    rows = below.shape[0]
    tile = pl.BlockSpec((TILE, WIDTH), lambda i, ends: (i, 0))
    half = pl.BlockSpec((BLOCK, WIDTH), lambda i, ends: (0, 0))
    return pl.pallas_call(
        raw_turn_kernel,
        grid_spec=pltpu.PrefetchScalarGridSpec(
            num_scalar_prefetch=1,
            grid=(rows // TILE,),
            in_specs=[tile, tile, tile] + [half] * 4,
            out_specs=[tile, pl.BlockSpec((3 * BLOCK, BLOCK), lambda i, ends: (0, 0))],
            scratch_shapes=[pltpu.VMEM((WIDTH, WIDTH), F32)] * 2,
        ),
        out_shape=[
            jax.ShapeDtypeStruct((rows, WIDTH), F32),
            jax.ShapeDtypeStruct((3 * BLOCK, BLOCK), F32),
        ],
        compiler_params=grant(12),
        cost_estimate=cost(2 * rows),
        name="raw_turn",
    )(ends, below, above, own, *rotations_t)


def last_turn_kernel(ends, one_ref, two_ref, raw_ref, *refs):
    main_refs, rest_refs, (out_ref, rows_ref, turned_ref, sems, out_sems) = refs[:4], refs[4:8], refs[8:]
    for tile in range(RAW // TILE):
        for column in range(2):
            half = raw_ref.at[:, pl.ds(column * BLOCK, BLOCK)]
            half_copies(half, rows_ref, sems, tile, 0, column).start()
    start_moved(ends, main_refs, rows_ref, sems, RAW // TILE)
    start_moved(ends, rest_refs, rows_ref, sems, (RAW + MAIN) // TILE)

    def out_copy(tile):
        rows = pl.ds(pl.multiple_of(tile * TILE, TILE), TILE)
        return pltpu.make_async_copy(turned_ref.at[rows, :], out_ref.at[rows, :], out_sems.at[tile])

    tiles = rows_ref.shape[0] // TILE
    rotation_t = jnp.concatenate([one_ref[...], two_ref[...]])

    @pl.loop(0, tiles)
    def _(tile):
        rows = wait_tile(main_refs[0], rows_ref, sems, tile)
        turned_ref[pl.ds(pl.multiple_of(tile * TILE, TILE), TILE), :] = product(rows, rotation_t)
        out_copy(tile).start()

    @pl.loop(0, tiles)
    def _(tile):
        out_copy(tile).wait()


def last_turn(ends, rotation_t, raw, main, rest):
    rows = raw.shape[0] + main[0].shape[0] + rest[0].shape[0]
    return pl.pallas_call(
        last_turn_kernel,
        in_specs=[pl.BlockSpec(memory_space=pltpu.SMEM)]
        + [pl.BlockSpec(memory_space=pltpu.VMEM)] * 2
        + [pl.BlockSpec(memory_space=pl.ANY)] * 9,
        out_specs=pl.BlockSpec(memory_space=pl.ANY),
        out_shape=jax.ShapeDtypeStruct((rows, WIDTH), F32),
        scratch_shapes=[pltpu.VMEM((rows, WIDTH), F32)] * 2
        + [pltpu.SemaphoreType.DMA((2, rows // TILE)), pltpu.SemaphoreType.DMA((rows // TILE,))],
        compiler_params=grant(24),
        cost_estimate=cost(rows),
        name="last_turn",
    )(ends, *rotation_t, raw, *main, *rest)


def send_up(value):
    count = lax.axis_size("col")
    return lax.ppermute(value, "col", [(p, p + 1) for p in range(count - 1)])


def send_down(value):
    count = lax.axis_size("col")
    return lax.ppermute(value, "col", [(p, p - 1) for p in range(1, count)])


def local(diffs, pairing):
    col_count = lax.axis_size("col")
    position = lax.axis_index("col")
    local_rows = diffs.shape[0]
    rows = col_count * local_rows
    bottom, top = position == 0, position == col_count - 1
    ends = jnp.stack([bottom, top]).astype(jnp.int32)
    ordered = order_pairs(diffs, pairing)
    pair_rows = lax.all_to_all(ordered, "col", split_axis=0, concat_axis=0, tiled=True)
    pair_rows = pair_rows.reshape(rows, WIDTH)

    parts = row_parts(local_gram(pair_rows))
    *parts, own = lax.optimization_barrier((*parts, pair_rows[:RAW]))
    below, above = send_up(own), send_down(own)
    first_t, second_t = pair_rotation(ends[:1], parts)
    sent = (below, above, send_up(first_t), send_down(second_t))
    moved = []
    for start, end in ((RAW, RAW + MAIN), (RAW + MAIN, rows)):
        first, second = turn(pair_rows, (first_t, second_t), start, end)
        if start == RAW:
            first, second, *sent = lax.optimization_barrier((first, second, *sent))
        moved.append((send_up(first), second, send_down(second), first))
    below, above, below_t, above_t = sent
    raw, gram = raw_turn(ends, below, above, own, first_t, second_t, below_t, above_t)
    for part in moved:
        gram = moved_gram(ends, gram, part)
    rotation_t = pair_rotation(jnp.zeros((1,), jnp.int32), row_parts(gram))
    return last_turn(ends, rotation_t, raw, *moved).reshape(col_count, 1, local_rows, WIDTH)


def solution(mesh):
    in_specs = (P(("col", "row"), None), P())
    out_specs = P(None, "row", None, "col")
    return jax.shard_map(local, mesh=mesh, in_specs=in_specs, out_specs=out_specs, check_vma=False)
```

```python
import functools

import jax
import jax.numpy as jnp
from jax import lax
from jax.experimental import pallas as pl
from jax.experimental.pallas import tpu as pltpu
from jax.sharding import PartitionSpec as P

BLOCK = 128
WIDTH = 2 * BLOCK
TILE = 1024
CHUNKS = (5 * TILE, 2 * TILE)
STRIP = 64
PANEL = 32
SUB = 8
HIGHEST = lax.Precision.HIGHEST
COLUMNS = (((0,), (0,)), ((), ()))
LANES = (((1,), (1,)), ((), ()))
F32 = jnp.float32
BF16 = jnp.bfloat16


def grant(megabytes):
    return pltpu.CompilerParams(vmem_limit_bytes=megabytes << 20)


def in_hbm(value):
    return pltpu.with_memory_space_constraint(value, pltpu.HBM)


def two_terms(value):
    high = value.astype(BF16)
    return high, (value - high.astype(F32)).astype(BF16)


def three_terms(value):
    high = value.astype(BF16)
    rest = value - high.astype(F32)
    middle = rest.astype(BF16)
    return high, middle, (rest - middle.astype(F32)).astype(BF16)


def order_kernel(pairing_ref, diffs_ref, out_ref, rows_ref, sems):
    strips = rows_ref.shape[0] // STRIP

    def strip_copy(strip):
        rows = pl.ds(pl.multiple_of(strip * STRIP, STRIP), STRIP)
        return pltpu.make_async_copy(diffs_ref.at[rows, :], rows_ref.at[rows, :], sems.at[strip])

    for strip in range(strips):
        strip_copy(strip).start()

    @pl.loop(0, strips)
    def _(strip):
        strip_copy(strip).wait()
        rows = pl.ds(pl.multiple_of(strip * STRIP, STRIP), STRIP)

        @pl.loop(0, out_ref.shape[0])
        def _(pair):
            for half in range(2):
                column = pl.multiple_of(pairing_ref[2 * pair + half] * BLOCK, BLOCK)
                block = rows_ref[rows, pl.ds(column, BLOCK)]
                out_ref[pair, rows, half * BLOCK : (half + 1) * BLOCK] = block


def order_pairs(diffs, pairing):
    rows, columns = diffs.shape
    return pl.pallas_call(
        order_kernel,
        in_specs=[
            pl.BlockSpec(memory_space=pltpu.SMEM),
            pl.BlockSpec(memory_space=pltpu.HBM),
        ],
        out_specs=pl.BlockSpec(memory_space=pltpu.VMEM),
        out_shape=jax.ShapeDtypeStruct((columns // WIDTH, rows, WIDTH), F32),
        scratch_shapes=[
            pltpu.VMEM((rows, columns), F32),
            pltpu.SemaphoreType.DMA((rows // STRIP,)),
        ],
        compiler_params=grant(24),
        name="order",
    )(pairing, in_hbm(diffs))


def add_gram(tile, total_ref, cross_ref):
    high, low = two_terms(tile)
    total_ref[...] += lax.dot_general(high, high, COLUMNS, preferred_element_type=F32)
    cross_ref[...] += lax.dot_general(high, low, COLUMNS, preferred_element_type=F32)


def row_copy(source_ref, rows_ref, sems, tile, first=0):
    source = source_ref.at[pl.ds(pl.multiple_of((tile + first) * TILE, TILE), TILE), :]
    rows = rows_ref.at[pl.ds(pl.multiple_of(tile * TILE, TILE), TILE), :]
    return pltpu.make_async_copy(source, rows, sems.at[tile])


def pack(total_ref, cross_ref):
    gram = total_ref[...] + (cross_ref[...] + cross_ref[...].T)
    return jnp.concatenate([gram[:BLOCK, :BLOCK], gram[:BLOCK, BLOCK:], gram[BLOCK:, BLOCK:]])


def unpack(packed):
    corner, side, end = packed[:BLOCK], packed[BLOCK : 2 * BLOCK], packed[2 * BLOCK :]
    upper = jnp.concatenate([corner, side], axis=1)
    return jnp.concatenate([upper, jnp.concatenate([side.T, end], axis=1)])


def gram_kernel(source_ref, out_ref, total_ref, cross_ref, rows_ref, sems):
    tiles = rows_ref.shape[0] // TILE
    for tile in range(tiles):
        row_copy(source_ref, rows_ref, sems, tile).start()
    total_ref[...] = jnp.zeros_like(total_ref)
    cross_ref[...] = jnp.zeros_like(cross_ref)

    @pl.loop(0, tiles)
    def _(tile):
        row_copy(source_ref, rows_ref, sems, tile).wait()
        rows = rows_ref[pl.ds(pl.multiple_of(tile * TILE, TILE), TILE), :]
        add_gram(rows, total_ref, cross_ref)

    out_ref[...] = pack(total_ref, cross_ref)


def local_gram(pair_rows):
    rows = pair_rows.shape[0]
    whole = pl.BlockSpec(memory_space=pltpu.VMEM)
    return pl.pallas_call(
        gram_kernel,
        in_specs=[pl.BlockSpec(memory_space=pltpu.HBM)],
        out_specs=whole,
        out_shape=jax.ShapeDtypeStruct((3 * BLOCK, BLOCK), F32),
        scratch_shapes=[
            pltpu.VMEM((WIDTH, WIDTH), F32),
            pltpu.VMEM((WIDTH, WIDTH), F32),
            pltpu.VMEM((rows, WIDTH), F32),
            pltpu.SemaphoreType.DMA((rows // TILE,)),
        ],
        compiler_params=grant(14),
        cost_estimate=pl.CostEstimate(flops=1000, bytes_accessed=1000, transcendentals=0),
        name="gram",
    )(in_hbm(pair_rows))


def cost(rows):
    return pl.CostEstimate(
        flops=6 * rows * WIDTH * WIDTH, bytes_accessed=8 * rows * WIDTH, transcendentals=0
    )


def moved_rows(ends, moved_refs, start, count):
    rows = pl.ds(start, count)
    below, second, above, first = (ref[rows, :] for ref in moved_refs)
    upper = jnp.where(ends[0] == 1, second, below)
    lower = jnp.where(ends[1] == 1, first, above)
    return upper, lower


def moved_tile(ends, moved_refs, tile):
    upper, lower = moved_rows(ends, moved_refs, pl.multiple_of(tile * TILE, TILE), TILE)
    return jnp.concatenate([upper, lower], axis=1)


def moved_gram_kernel(ends, before_ref, *refs):
    moved_refs, (out_ref, total_ref, cross_ref) = refs[:4], refs[4:]
    total_ref[...] = jnp.zeros_like(total_ref)
    cross_ref[...] = jnp.zeros_like(cross_ref)

    @pl.loop(0, moved_refs[0].shape[0] // TILE)
    def _(tile):
        add_gram(moved_tile(ends, moved_refs, tile), total_ref, cross_ref)

    out_ref[...] = before_ref[...] + pack(total_ref, cross_ref)


def in_vmem(count):
    whole = pl.BlockSpec(memory_space=pltpu.VMEM)
    return [pl.BlockSpec(memory_space=pltpu.SMEM)] + [whole] * count


def moved_gram(ends, before, moved):
    return pl.pallas_call(
        moved_gram_kernel,
        in_specs=in_vmem(5),
        out_specs=pl.BlockSpec(memory_space=pltpu.VMEM),
        out_shape=jax.ShapeDtypeStruct((3 * BLOCK, BLOCK), F32),
        scratch_shapes=[pltpu.VMEM((WIDTH, WIDTH), F32)] * 2,
        compiler_params=grant(24),
        cost_estimate=cost(moved[0].shape[0]),
        name="moved_gram",
    )(ends, before, *moved)


def row_parts(packed):
    count = lax.axis_size("row")
    step = 1
    while True:
        swap = [(source, source ^ step) for source in range(count)]
        parts = (packed, lax.ppermute(packed, "row", swap))
        step *= 2
        if step >= count:
            return parts
        packed = parts[0] + parts[1]


def outer_product(left, right):
    left1, left2, left3 = three_terms(left)
    right1, right2, right3 = three_terms(right)
    left = jnp.concatenate([left1, left1, left2, left2, left1, left3], axis=0)
    right = jnp.concatenate([right1, right2, right1, right2, right3, right1], axis=0)
    return lax.dot_general(left, right, COLUMNS, preferred_element_type=F32)


def spread(value):
    return jnp.broadcast_to(value, (SUB, BLOCK))


def total(terms):
    while len(terms) > 1:
        paired = [a + b for a, b in zip(terms[::2], terms[1::2])]
        terms = paired + terms[len(terms) - len(terms) % 2 :]
    return terms[0]


def small_inverse(tile, lane, spread_ref, base):
    for j in range(SUB):
        spread_ref[base + SUB * j : base + SUB * (j + 1), :] = spread(tile[:, lane + j : lane + j + 1])
    entry = {
        (i, j): spread_ref[pl.ds(base + SUB * j + i, SUB, stride=0), :]
        for j in range(SUB)
        for i in range(j, SUB)
    }
    lower, scales = {}, []
    for j in range(SUB):
        scale = lax.rsqrt(entry[j, j])
        inverse = scale * scale
        scales.append(scale)
        for i in range(j + 1, SUB):
            lower[i, j] = entry[i, j] * inverse
        for m in range(j + 1, SUB):
            for i in range(m, SUB):
                entry[i, m] = entry[i, m] - lower[i, j] * entry[m, j]
    solved = {}
    for j in range(SUB):
        for i in range(j + 1, SUB):
            terms = [lower[i, j]] + [lower[i, m] * solved[m, j] for m in range(j + 1, i)]
            solved[i, j] = -total(terms)
    solved = {at: value * scales[at[0]] for at, value in solved.items()}
    return solved | {(j, j): scales[j] for j in range(SUB)}


def tiles_of(ref, start, end, first, last):
    return jnp.concatenate([ref[t, start:end, :] for t in range(first, last)], axis=1)


def put_tiles(ref, first, value):
    for t in range(value.shape[1] // BLOCK):
        ref[first + t] = value[:, BLOCK * t : BLOCK * (t + 1)]


def eliminate(work_ref, factor_ref, spread_ref, tiles):
    row = lax.broadcasted_iota(jnp.int32, (SUB, BLOCK), 0)
    lane = lax.broadcasted_iota(jnp.int32, (SUB, BLOCK), 1)
    zero = jnp.zeros((SUB, BLOCK), F32)
    for start in range(0, WIDTH, PANEL):
        end = start + PANEL
        own = start // BLOCK
        for top in range(start, end, SUB):
            at = top % BLOCK
            base = SUB * SUB * (top // SUB % 2)
            small = small_inverse(work_ref[own, top : top + SUB, :], at, spread_ref, base)
            columns = []
            for j in range(SUB):
                column = zero
                for i in range(j, SUB):
                    column = jnp.where(row == i, small[i, j], column)
                columns.append(column)
            for t in range(tiles):
                if t < own:
                    solved = zero
                else:
                    solved = total(
                        [columns[j] * work_ref[t, pl.ds(top + j, SUB, stride=0), :] for j in range(SUB)]
                    )
                    if t == own:
                        solved = jnp.where(lane >= row + at, solved, 0.0)
                factor_ref[t, top : top + SUB, :] = solved
            for below in range(top + SUB, end, SUB):
                tile = work_ref[own, below : below + SUB, :]
                entries = [spread(tile[:, at + j : at + j + 1]) for j in range(SUB)]
                left = [total([entries[j] * small[i, j] for j in range(i + 1)]) for i in range(SUB)]
                for t in range(own, tiles):
                    work_ref[t, below : below + SUB, :] -= total(
                        [left[i] * factor_ref[t, pl.ds(top + i, SUB, stride=0), :] for i in range(SUB)]
                    )
        if end < WIDTH:
            first = end // BLOCK
            update = outer_product(
                tiles_of(factor_ref, start, end, first, WIDTH // BLOCK),
                tiles_of(factor_ref, start, end, first, tiles),
            )
            for t in range(first, tiles):
                here = BLOCK * (t - first)
                work_ref[t, end:, :] -= update[end - BLOCK * first :, here : here + BLOCK]


def rotation_kernel(swap_ref, one_ref, two_ref, first_ref, second_ref, work_ref, factor_ref, spread_ref):
    gram = unpack(one_ref[...] + two_ref[...])
    square = jnp.dot(gram, gram, precision=HIGHEST, preferred_element_type=F32)
    put_tiles(work_ref, 0, square)
    eliminate(work_ref, factor_ref, spread_ref, WIDTH // BLOCK)
    factor = tiles_of(factor_ref, 0, WIDTH, 0, WIDTH // BLOCK)
    square = lax.dot_general(factor, factor, LANES, precision=HIGHEST, preferred_element_type=F32)
    put_tiles(work_ref, 0, square)
    put_tiles(work_ref, WIDTH // BLOCK, factor)
    eliminate(work_ref, factor_ref, spread_ref, 2 * WIDTH // BLOCK)
    halves = [
        tiles_of(factor_ref, start, start + BLOCK, WIDTH // BLOCK, 2 * WIDTH // BLOCK)
        for start in (0, BLOCK)
    ]
    first_ref[...] = jnp.where(swap_ref[0] == 1, halves[1], halves[0])
    second_ref[...] = jnp.where(swap_ref[0] == 1, halves[0], halves[1])


def pair_rotation(swap, parts):
    tiles = pltpu.VMEM((2 * WIDTH // BLOCK, WIDTH, BLOCK), F32)
    return pl.pallas_call(
        rotation_kernel,
        in_specs=[pl.BlockSpec(memory_space=pltpu.SMEM)] + [pl.BlockSpec(memory_space=pltpu.VMEM)] * 2,
        out_shape=[jax.ShapeDtypeStruct((BLOCK, WIDTH), F32)] * 2,
        scratch_shapes=[tiles, tiles, pltpu.VMEM((2 * SUB * SUB, BLOCK), F32)],
        compiler_params=grant(8),
        cost_estimate=pl.CostEstimate(flops=1000, bytes_accessed=1000, transcendentals=0),
        name="rotation",
    )(swap, *parts)


def product(rows, rotation_t):
    high, low = two_terms(rows)
    turn_high, turn_low = two_terms(rotation_t)
    turned = lax.dot_general(high, turn_high, LANES, preferred_element_type=F32)
    turned += lax.dot_general(low, turn_high, LANES, preferred_element_type=F32)
    return turned + lax.dot_general(high, turn_low, LANES, preferred_element_type=F32)


def turn_kernel(start, source_ref, one_ref, two_ref, first_ref, second_ref, rows_ref, sems):
    tiles = rows_ref.shape[0] // TILE
    for tile in range(tiles):
        row_copy(source_ref, rows_ref, sems, tile, start // TILE).start()
    rotation_t = jnp.concatenate([one_ref[...], two_ref[...]])
    if first_ref.shape[0] > rows_ref.shape[0]:
        for half_ref, out_ref in ((one_ref, first_ref), (two_ref, second_ref)):
            end = rows_ref.shape[0]
            out_ref[end : end + BLOCK, :] = half_ref[:, :BLOCK]
            out_ref[end + BLOCK :, :] = half_ref[:, BLOCK:]

    @pl.loop(0, tiles)
    def _(tile):
        row_copy(source_ref, rows_ref, sems, tile, start // TILE).wait()
        rows = pl.ds(pl.multiple_of(tile * TILE, TILE), TILE)
        turned = product(rows_ref[rows, :], rotation_t)
        first_ref[rows, :] = turned[:, :BLOCK]
        second_ref[rows, :] = turned[:, BLOCK:]


def turn(pair_rows, rotation_t, start, rows, extra):
    whole = pl.BlockSpec(memory_space=pltpu.VMEM)
    return pl.pallas_call(
        functools.partial(turn_kernel, start),
        in_specs=[pl.BlockSpec(memory_space=pltpu.HBM), whole, whole],
        out_specs=[whole, whole],
        out_shape=[jax.ShapeDtypeStruct((rows + extra, BLOCK), F32)] * 2,
        scratch_shapes=[
            pltpu.VMEM((rows, WIDTH), F32),
            pltpu.SemaphoreType.DMA((rows // TILE,)),
        ],
        compiler_params=grant(24),
        cost_estimate=cost(rows),
        name="turn",
    )(in_hbm(pair_rows), *rotation_t)


def raw_gram_kernel(ends, below_ref, above_ref, own_ref, *refs):
    moved_refs, (out_ref, packed_ref, total_ref, cross_ref) = refs[:4], refs[4:]
    total_ref[...] = jnp.zeros_like(total_ref)
    cross_ref[...] = jnp.zeros_like(cross_ref)
    halves_t = [
        jnp.concatenate([half[:BLOCK], half[BLOCK:]], axis=1)
        for half in moved_rows(ends, moved_refs, CHUNKS[0], WIDTH)
    ]
    own = own_ref[...]
    upper = product(jnp.where(ends[0] == 1, own, below_ref[...]), halves_t[0])
    lower = product(jnp.where(ends[1] == 1, own, above_ref[...]), halves_t[1])
    tile = jnp.concatenate([upper, lower], axis=1)
    out_ref[...] = tile
    add_gram(tile, total_ref, cross_ref)
    packed_ref[...] = pack(total_ref, cross_ref)


def raw_gram(ends, below, above, own, moved):
    whole = pl.BlockSpec(memory_space=pltpu.VMEM)
    return pl.pallas_call(
        raw_gram_kernel,
        in_specs=in_vmem(7),
        out_specs=[whole, whole],
        out_shape=[
            jax.ShapeDtypeStruct((TILE, WIDTH), F32),
            jax.ShapeDtypeStruct((3 * BLOCK, BLOCK), F32),
        ],
        scratch_shapes=[pltpu.VMEM((WIDTH, WIDTH), F32)] * 2,
        compiler_params=grant(24),
        cost_estimate=cost(2 * TILE),
        name="raw_gram",
    )(ends, below, above, own, *moved)


def last_turn_kernel(ends, one_ref, two_ref, raw_ref, *refs):
    moved, (out_ref, turned_ref, sems) = (refs[0:4], refs[4:8]), refs[8:]
    rotation_t = jnp.concatenate([one_ref[...], two_ref[...]])

    def out_copy(tile):
        rows = pl.ds(pl.multiple_of(tile * TILE, TILE), TILE)
        return pltpu.make_async_copy(turned_ref.at[rows, :], out_ref.at[rows, :], sems.at[tile])

    def put(tile, rows):
        turned_ref[pl.ds(pl.multiple_of(tile * TILE, TILE), TILE), :] = product(rows, rotation_t)
        out_copy(tile).start()

    put(0, raw_ref[...])
    done = 1
    for moved_refs, rows in zip(moved, CHUNKS):

        @pl.loop(0, rows // TILE)
        def _(tile, moved_refs=moved_refs, done=done):
            put(done + tile, moved_tile(ends, moved_refs, tile))

        done += rows // TILE

    @pl.loop(0, done)
    def _(tile):
        out_copy(tile).wait()


def last_turn(ends, rotation_t, raw, moved):
    rows = TILE + sum(CHUNKS)
    moved = [array for part in moved for array in part]
    return pl.pallas_call(
        last_turn_kernel,
        in_specs=in_vmem(3 + len(moved)),
        out_specs=pl.BlockSpec(memory_space=pl.ANY),
        out_shape=jax.ShapeDtypeStruct((rows, WIDTH), F32),
        scratch_shapes=[
            pltpu.VMEM((rows, WIDTH), F32),
            pltpu.SemaphoreType.DMA((rows // TILE,)),
        ],
        compiler_params=grant(24),
        cost_estimate=cost(rows),
        name="last_turn",
    )(ends, *rotation_t, raw, *moved)


def send_up(value):
    count = lax.axis_size("col")
    return lax.ppermute(value, "col", [(p, p + 1) for p in range(count - 1)])


def send_down(value):
    count = lax.axis_size("col")
    return lax.ppermute(value, "col", [(p, p - 1) for p in range(1, count)])


def local(diffs, pairing):
    col_count = lax.axis_size("col")
    position = lax.axis_index("col")
    local_rows = diffs.shape[0]
    rows = col_count * local_rows
    bottom, top = position == 0, position == col_count - 1
    ends = jnp.stack([bottom, top]).astype(jnp.int32)
    ordered = order_pairs(diffs, pairing)
    pair_rows = lax.all_to_all(ordered, "col", split_axis=0, concat_axis=0, tiled=True)
    pair_rows = pair_rows.reshape(rows, WIDTH)

    parts = row_parts(local_gram(pair_rows))
    *parts, own = lax.optimization_barrier((*parts, pair_rows[:TILE]))
    below, above = send_up(own), send_down(own)
    rotation_t = pair_rotation(ends[:1], parts)
    moved, start = [], TILE
    for chunk, count in enumerate(CHUNKS):
        first, second = turn(pair_rows, rotation_t, start, count, 0 if chunk else WIDTH)
        if chunk == 0:
            first, second, below, above = lax.optimization_barrier((first, second, below, above))
        moved.append((send_up(first), second, send_down(second), first))
        start += count
    raw, gram = raw_gram(ends, below, above, own, moved[0])
    for part in moved:
        gram = moved_gram(ends, gram, part)
    rotation_t = pair_rotation(jnp.zeros((1,), jnp.int32), row_parts(gram))
    return last_turn(ends, rotation_t, raw, moved).reshape(col_count, 1, local_rows, WIDTH)


def solution(mesh):
    in_specs = (P(("col", "row"), None), P())
    out_specs = P(None, "row", None, "col")
    return jax.shard_map(local, mesh=mesh, in_specs=in_specs, out_specs=out_specs, check_vma=False)
```

```python
import functools

import jax
import jax.numpy as jnp
from jax import lax
from jax.experimental import pallas as pl
from jax.experimental.pallas import tpu as pltpu
from jax.sharding import PartitionSpec as P

BLOCK = 128
WIDTH = 2 * BLOCK
TILE = 1024
RAW = 1536
CHUNKS = (4608, 2048)
STRIP = 64
PANEL = 32
SUB = 8
HIGHEST = lax.Precision.HIGHEST
COLUMNS = (((0,), (0,)), ((), ()))
LANES = (((1,), (1,)), ((), ()))
F32 = jnp.float32
BF16 = jnp.bfloat16


def grant(megabytes):
    return pltpu.CompilerParams(vmem_limit_bytes=megabytes << 20)


def in_hbm(value):
    return pltpu.with_memory_space_constraint(value, pltpu.HBM)


def two_terms(value):
    high = value.astype(BF16)
    return high, (value - high.astype(F32)).astype(BF16)


def three_terms(value):
    high = value.astype(BF16)
    rest = value - high.astype(F32)
    middle = rest.astype(BF16)
    return high, middle, (rest - middle.astype(F32)).astype(BF16)


def order_kernel(pairing_ref, diffs_ref, out_ref, rows_ref, sems):
    strips = rows_ref.shape[0] // STRIP

    def strip_copy(strip):
        rows = pl.ds(pl.multiple_of(strip * STRIP, STRIP), STRIP)
        return pltpu.make_async_copy(diffs_ref.at[rows, :], rows_ref.at[rows, :], sems.at[strip])

    for strip in range(strips):
        strip_copy(strip).start()

    @pl.loop(0, strips)
    def _(strip):
        strip_copy(strip).wait()
        rows = pl.ds(pl.multiple_of(strip * STRIP, STRIP), STRIP)

        @pl.loop(0, out_ref.shape[0])
        def _(pair):
            for half in range(2):
                column = pl.multiple_of(pairing_ref[2 * pair + half] * BLOCK, BLOCK)
                block = rows_ref[rows, pl.ds(column, BLOCK)]
                out_ref[pair, rows, half * BLOCK : (half + 1) * BLOCK] = block


def order_pairs(diffs, pairing):
    rows, columns = diffs.shape
    return pl.pallas_call(
        order_kernel,
        in_specs=[
            pl.BlockSpec(memory_space=pltpu.SMEM),
            pl.BlockSpec(memory_space=pltpu.HBM),
        ],
        out_specs=pl.BlockSpec(memory_space=pltpu.VMEM),
        out_shape=jax.ShapeDtypeStruct((columns // WIDTH, rows, WIDTH), F32),
        scratch_shapes=[
            pltpu.VMEM((rows, columns), F32),
            pltpu.SemaphoreType.DMA((rows // STRIP,)),
        ],
        compiler_params=grant(24),
        name="order",
    )(pairing, in_hbm(diffs))


def add_gram(tile, total_ref, cross_ref):
    high, low = two_terms(tile)
    total_ref[...] += lax.dot_general(high, high, COLUMNS, preferred_element_type=F32)
    cross_ref[...] += lax.dot_general(high, low, COLUMNS, preferred_element_type=F32)


def for_tiles(rows, body):
    tiles, rest = divmod(rows, TILE)

    @pl.loop(0, tiles)
    def _(tile):
        body(pl.multiple_of(tile * TILE, TILE), TILE, tile)

    if rest:
        body(tiles * TILE, rest, tiles)


def row_copy(source_ref, rows_ref, sems, row, size, tile, start=0):
    source = source_ref.at[pl.ds(pl.multiple_of(row + start, BLOCK), size), :]
    return pltpu.make_async_copy(source, rows_ref.at[pl.ds(row, size), :], sems.at[tile])


def start_rows(source_ref, rows_ref, sems, start=0):
    for tile, row in enumerate(range(0, rows_ref.shape[0], TILE)):
        size = min(TILE, rows_ref.shape[0] - row)
        row_copy(source_ref, rows_ref, sems, row, size, tile, start).start()


def pack(total_ref, cross_ref):
    gram = total_ref[...] + (cross_ref[...] + cross_ref[...].T)
    return jnp.concatenate([gram[:BLOCK, :BLOCK], gram[:BLOCK, BLOCK:], gram[BLOCK:, BLOCK:]])


def unpack(packed):
    corner, side, end = packed[:BLOCK], packed[BLOCK : 2 * BLOCK], packed[2 * BLOCK :]
    upper = jnp.concatenate([corner, side], axis=1)
    return jnp.concatenate([upper, jnp.concatenate([side.T, end], axis=1)])


def gram_kernel(source_ref, out_ref, total_ref, cross_ref, rows_ref, sems):
    start_rows(source_ref, rows_ref, sems)
    total_ref[...] = jnp.zeros_like(total_ref)
    cross_ref[...] = jnp.zeros_like(cross_ref)

    def add(row, size, tile):
        row_copy(source_ref, rows_ref, sems, row, size, tile).wait()
        add_gram(rows_ref[pl.ds(row, size), :], total_ref, cross_ref)

    for_tiles(rows_ref.shape[0], add)
    out_ref[...] = pack(total_ref, cross_ref)


def local_gram(pair_rows):
    rows = pair_rows.shape[0]
    whole = pl.BlockSpec(memory_space=pltpu.VMEM)
    return pl.pallas_call(
        gram_kernel,
        in_specs=[pl.BlockSpec(memory_space=pltpu.HBM)],
        out_specs=whole,
        out_shape=jax.ShapeDtypeStruct((3 * BLOCK, BLOCK), F32),
        scratch_shapes=[
            pltpu.VMEM((WIDTH, WIDTH), F32),
            pltpu.VMEM((WIDTH, WIDTH), F32),
            pltpu.VMEM((rows, WIDTH), F32),
            pltpu.SemaphoreType.DMA((rows // TILE,)),
        ],
        compiler_params=grant(14),
        cost_estimate=pl.CostEstimate(flops=1000, bytes_accessed=1000, transcendentals=0),
        name="gram",
    )(in_hbm(pair_rows))


def cost(rows):
    return pl.CostEstimate(
        flops=6 * rows * WIDTH * WIDTH, bytes_accessed=8 * rows * WIDTH, transcendentals=0
    )


def moved_rows(ends, moved_refs, start, count):
    rows = pl.ds(start, count)
    below, second, above, first = (ref[rows, :] for ref in moved_refs)
    upper = jnp.where(ends[0] == 1, second, below)
    lower = jnp.where(ends[1] == 1, first, above)
    return upper, lower


def moved_tile(ends, moved_refs, row, size):
    return jnp.concatenate(moved_rows(ends, moved_refs, row, size), axis=1)


def moved_gram_kernel(rows, ends, before_ref, *refs):
    moved_refs, (out_ref, total_ref, cross_ref) = refs[:4], refs[4:]
    total_ref[...] = jnp.zeros_like(total_ref)
    cross_ref[...] = jnp.zeros_like(cross_ref)

    def add(row, size, tile):
        add_gram(moved_tile(ends, moved_refs, row, size), total_ref, cross_ref)

    for_tiles(rows, add)

    out_ref[...] = before_ref[...] + pack(total_ref, cross_ref)


def in_vmem(count):
    whole = pl.BlockSpec(memory_space=pltpu.VMEM)
    return [pl.BlockSpec(memory_space=pltpu.SMEM)] + [whole] * count


def moved_gram(ends, before, moved, chunk):
    return pl.pallas_call(
        functools.partial(moved_gram_kernel, chunk),
        in_specs=in_vmem(5),
        out_specs=pl.BlockSpec(memory_space=pltpu.VMEM),
        out_shape=jax.ShapeDtypeStruct((3 * BLOCK, BLOCK), F32),
        scratch_shapes=[pltpu.VMEM((WIDTH, WIDTH), F32)] * 2,
        compiler_params=grant(24),
        cost_estimate=cost(chunk),
        name="moved_gram",
    )(ends, before, *moved)


def row_parts(packed):
    count = lax.axis_size("row")
    step = 1
    while True:
        swap = [(source, source ^ step) for source in range(count)]
        parts = (packed, lax.ppermute(packed, "row", swap))
        step *= 2
        if step >= count:
            return parts
        packed = parts[0] + parts[1]


def outer_product(left, right):
    left1, left2, left3 = three_terms(left)
    right1, right2, right3 = three_terms(right)
    left = jnp.concatenate([left1, left1, left2, left2, left1, left3], axis=0)
    right = jnp.concatenate([right1, right2, right1, right2, right3, right1], axis=0)
    return lax.dot_general(left, right, COLUMNS, preferred_element_type=F32)


def spread(value):
    return jnp.broadcast_to(value, (SUB, BLOCK))


def total(terms):
    while len(terms) > 1:
        paired = [a + b for a, b in zip(terms[::2], terms[1::2])]
        terms = paired + terms[len(terms) - len(terms) % 2 :]
    return terms[0]


def small_inverse(tile, lane, spread_ref, base):
    for j in range(SUB):
        spread_ref[base + SUB * j : base + SUB * (j + 1), :] = spread(tile[:, lane + j : lane + j + 1])
    entry = {
        (i, j): spread_ref[pl.ds(base + SUB * j + i, SUB, stride=0), :]
        for j in range(SUB)
        for i in range(j, SUB)
    }
    lower, scales = {}, []
    for j in range(SUB):
        scale = lax.rsqrt(entry[j, j])
        inverse = scale * scale
        scales.append(scale)
        for i in range(j + 1, SUB):
            lower[i, j] = entry[i, j] * inverse
        for m in range(j + 1, SUB):
            for i in range(m, SUB):
                entry[i, m] = entry[i, m] - lower[i, j] * entry[m, j]
    solved = {}
    for j in range(SUB):
        for i in range(j + 1, SUB):
            terms = [lower[i, j]] + [lower[i, m] * solved[m, j] for m in range(j + 1, i)]
            solved[i, j] = -total(terms)
    solved = {at: value * scales[at[0]] for at, value in solved.items()}
    return solved | {(j, j): scales[j] for j in range(SUB)}


def tiles_of(ref, start, end, first, last):
    return jnp.concatenate([ref[t, start:end, :] for t in range(first, last)], axis=1)


def put_tiles(ref, first, value):
    for t in range(value.shape[1] // BLOCK):
        ref[first + t] = value[:, BLOCK * t : BLOCK * (t + 1)]


def eliminate(work_ref, factor_ref, spread_ref, tiles):
    row = lax.broadcasted_iota(jnp.int32, (SUB, BLOCK), 0)
    lane = lax.broadcasted_iota(jnp.int32, (SUB, BLOCK), 1)
    zero = jnp.zeros((SUB, BLOCK), F32)
    for start in range(0, WIDTH, PANEL):
        end = start + PANEL
        own = start // BLOCK
        for top in range(start, end, SUB):
            at = top % BLOCK
            base = SUB * SUB * (top // SUB % 2)
            small = small_inverse(work_ref[own, top : top + SUB, :], at, spread_ref, base)
            columns = []
            for j in range(SUB):
                column = zero
                for i in range(j, SUB):
                    column = jnp.where(row == i, small[i, j], column)
                columns.append(column)
            for t in range(tiles):
                if t < own:
                    solved = zero
                else:
                    solved = total(
                        [columns[j] * work_ref[t, pl.ds(top + j, SUB, stride=0), :] for j in range(SUB)]
                    )
                    if t == own:
                        solved = jnp.where(lane >= row + at, solved, 0.0)
                factor_ref[t, top : top + SUB, :] = solved
            for below in range(top + SUB, end, SUB):
                tile = work_ref[own, below : below + SUB, :]
                entries = [spread(tile[:, at + j : at + j + 1]) for j in range(SUB)]
                left = [total([entries[j] * small[i, j] for j in range(i + 1)]) for i in range(SUB)]
                for t in range(own, tiles):
                    work_ref[t, below : below + SUB, :] -= total(
                        [left[i] * factor_ref[t, pl.ds(top + i, SUB, stride=0), :] for i in range(SUB)]
                    )
        if end < WIDTH:
            first = end // BLOCK
            update = outer_product(
                tiles_of(factor_ref, start, end, first, WIDTH // BLOCK),
                tiles_of(factor_ref, start, end, first, tiles),
            )
            for t in range(first, tiles):
                here = BLOCK * (t - first)
                work_ref[t, end:, :] -= update[end - BLOCK * first :, here : here + BLOCK]


def rotation_kernel(swap_ref, one_ref, two_ref, first_ref, second_ref, work_ref, factor_ref, spread_ref):
    gram = unpack(one_ref[...] + two_ref[...])
    square = jnp.dot(gram, gram, precision=HIGHEST, preferred_element_type=F32)
    put_tiles(work_ref, 0, square)
    eliminate(work_ref, factor_ref, spread_ref, WIDTH // BLOCK)
    factor = tiles_of(factor_ref, 0, WIDTH, 0, WIDTH // BLOCK)
    square = lax.dot_general(factor, factor, LANES, precision=HIGHEST, preferred_element_type=F32)
    put_tiles(work_ref, 0, square)
    put_tiles(work_ref, WIDTH // BLOCK, factor)
    eliminate(work_ref, factor_ref, spread_ref, 2 * WIDTH // BLOCK)
    halves = [
        tiles_of(factor_ref, start, start + BLOCK, WIDTH // BLOCK, 2 * WIDTH // BLOCK)
        for start in (0, BLOCK)
    ]
    first_ref[...] = jnp.where(swap_ref[0] == 1, halves[1], halves[0])
    second_ref[...] = jnp.where(swap_ref[0] == 1, halves[0], halves[1])


def pair_rotation(swap, parts):
    tiles = pltpu.VMEM((2 * WIDTH // BLOCK, WIDTH, BLOCK), F32)
    return pl.pallas_call(
        rotation_kernel,
        in_specs=[pl.BlockSpec(memory_space=pltpu.SMEM)] + [pl.BlockSpec(memory_space=pltpu.VMEM)] * 2,
        out_shape=[jax.ShapeDtypeStruct((BLOCK, WIDTH), F32)] * 2,
        scratch_shapes=[tiles, tiles, pltpu.VMEM((2 * SUB * SUB, BLOCK), F32)],
        compiler_params=grant(8),
        cost_estimate=pl.CostEstimate(flops=1000, bytes_accessed=1000, transcendentals=0),
        name="rotation",
    )(swap, *parts)


def product(rows, rotation_t):
    high, low = two_terms(rows)
    turn_high, turn_low = two_terms(rotation_t)
    turned = lax.dot_general(high, turn_high, LANES, preferred_element_type=F32)
    turned += lax.dot_general(low, turn_high, LANES, preferred_element_type=F32)
    return turned + lax.dot_general(high, turn_low, LANES, preferred_element_type=F32)


def turn_kernel(start, source_ref, one_ref, two_ref, first_ref, second_ref, rows_ref, sems):
    start_rows(source_ref, rows_ref, sems, start)
    rotation_t = jnp.concatenate([one_ref[...], two_ref[...]])
    if first_ref.shape[0] > rows_ref.shape[0]:
        for half_ref, out_ref in ((one_ref, first_ref), (two_ref, second_ref)):
            end = rows_ref.shape[0]
            out_ref[end : end + BLOCK, :] = half_ref[:, :BLOCK]
            out_ref[end + BLOCK :, :] = half_ref[:, BLOCK:]

    def put(row, size, tile):
        row_copy(source_ref, rows_ref, sems, row, size, tile, start).wait()
        rows = pl.ds(row, size)
        turned = product(rows_ref[rows, :], rotation_t)
        first_ref[rows, :] = turned[:, :BLOCK]
        second_ref[rows, :] = turned[:, BLOCK:]

    for_tiles(rows_ref.shape[0], put)


def turn(pair_rows, rotation_t, start, rows, extra):
    whole = pl.BlockSpec(memory_space=pltpu.VMEM)
    return pl.pallas_call(
        functools.partial(turn_kernel, start),
        in_specs=[pl.BlockSpec(memory_space=pltpu.HBM), whole, whole],
        out_specs=[whole, whole],
        out_shape=[jax.ShapeDtypeStruct((rows + extra, BLOCK), F32)] * 2,
        scratch_shapes=[
            pltpu.VMEM((rows, WIDTH), F32),
            pltpu.SemaphoreType.DMA((pl.cdiv(rows, TILE),)),
        ],
        compiler_params=grant(24),
        cost_estimate=cost(rows if extra else 1000 * rows),
        name="turn",
    )(in_hbm(pair_rows), *rotation_t)


def raw_gram_kernel(ends, below_ref, above_ref, own_ref, *refs):
    moved_refs, (out_ref, packed_ref, total_ref, cross_ref) = refs[:4], refs[4:]
    total_ref[...] = jnp.zeros_like(total_ref)
    cross_ref[...] = jnp.zeros_like(cross_ref)
    halves_t = [
        jnp.concatenate([half[:BLOCK], half[BLOCK:]], axis=1)
        for half in moved_rows(ends, moved_refs, CHUNKS[0], WIDTH)
    ]

    def put(row, size, tile):
        rows = pl.ds(row, size)
        own = own_ref[rows, :]
        upper = product(jnp.where(ends[0] == 1, own, below_ref[rows, :]), halves_t[0])
        lower = product(jnp.where(ends[1] == 1, own, above_ref[rows, :]), halves_t[1])
        turned = jnp.concatenate([upper, lower], axis=1)
        out_ref[rows, :] = turned
        add_gram(turned, total_ref, cross_ref)

    for_tiles(RAW, put)
    packed_ref[...] = pack(total_ref, cross_ref)


def raw_gram(ends, below, above, own, moved):
    whole = pl.BlockSpec(memory_space=pltpu.VMEM)
    return pl.pallas_call(
        raw_gram_kernel,
        in_specs=in_vmem(7),
        out_specs=[whole, whole],
        out_shape=[
            jax.ShapeDtypeStruct((RAW, WIDTH), F32),
            jax.ShapeDtypeStruct((3 * BLOCK, BLOCK), F32),
        ],
        scratch_shapes=[pltpu.VMEM((WIDTH, WIDTH), F32)] * 2,
        compiler_params=grant(24),
        cost_estimate=cost(2 * RAW),
        name="raw_gram",
    )(ends, below, above, own, *moved)


def last_turn_kernel(ends, one_ref, two_ref, raw_ref, *refs):
    moved, (out_ref, turned_ref, sems) = (refs[0:4], refs[4:8]), refs[8:]
    rotation_t = jnp.concatenate([one_ref[...], two_ref[...]])

    def out_copy(row, size, sem):
        rows = pl.ds(pl.multiple_of(row, BLOCK), size)
        return pltpu.make_async_copy(turned_ref.at[rows, :], out_ref.at[rows, :], sems.at[sem])

    start, sem = 0, 0
    copies = []
    for moved_refs, count in zip((None, *moved), (RAW, *CHUNKS)):

        def put(row, size, tile, moved_refs=moved_refs, start=start, sem=sem):
            if moved_refs is None:
                rows = raw_ref[pl.ds(row, size), :]
            else:
                rows = moved_tile(ends, moved_refs, row, size)
            at = pl.ds(pl.multiple_of(start + row, BLOCK), size)
            turned_ref[at, :] = product(rows, rotation_t)
            out_copy(start + row, size, sem + tile).start()

        for_tiles(count, put)
        for row in range(0, count, TILE):
            copies.append((start + row, min(TILE, count - row), sem))
            sem += 1
        start += count
    for copy in copies:
        out_copy(*copy).wait()


def last_turn(ends, rotation_t, raw, moved):
    rows = RAW + sum(CHUNKS)
    tiles = sum(pl.cdiv(count, TILE) for count in (RAW, *CHUNKS))
    moved = [array for part in moved for array in part]
    return pl.pallas_call(
        last_turn_kernel,
        in_specs=in_vmem(3 + len(moved)),
        out_specs=pl.BlockSpec(memory_space=pl.ANY),
        out_shape=jax.ShapeDtypeStruct((rows, WIDTH), F32),
        scratch_shapes=[
            pltpu.VMEM((rows, WIDTH), F32),
            pltpu.SemaphoreType.DMA((tiles,)),
        ],
        compiler_params=grant(24),
        cost_estimate=cost(rows),
        name="last_turn",
    )(ends, *rotation_t, raw, *moved)


def send_up(value):
    count = lax.axis_size("col")
    return lax.ppermute(value, "col", [(p, p + 1) for p in range(count - 1)])


def send_down(value):
    count = lax.axis_size("col")
    return lax.ppermute(value, "col", [(p, p - 1) for p in range(1, count)])


def local(diffs, pairing):
    col_count = lax.axis_size("col")
    position = lax.axis_index("col")
    local_rows = diffs.shape[0]
    rows = col_count * local_rows
    bottom, top = position == 0, position == col_count - 1
    ends = jnp.stack([bottom, top]).astype(jnp.int32)
    ordered = order_pairs(diffs, pairing)
    pair_rows = lax.all_to_all(ordered, "col", split_axis=0, concat_axis=0, tiled=True)
    pair_rows = pair_rows.reshape(rows, WIDTH)

    parts = row_parts(local_gram(pair_rows))
    *parts, own = lax.optimization_barrier((*parts, pair_rows[:RAW]))
    below, above = send_up(own), send_down(own)
    rotation_t = pair_rotation(ends[:1], parts)
    moved, start = [], RAW
    for number, chunk in enumerate(CHUNKS):
        first, second = turn(pair_rows, rotation_t, start, chunk, 0 if number else WIDTH)
        if number == 1:
            first, second, below, above = lax.optimization_barrier((first, second, below, above))
        moved.append((send_up(first), second, send_down(second), first))
        start += chunk
    raw, gram = raw_gram(ends, below, above, own, moved[0])
    for part, chunk in zip(moved, CHUNKS):
        gram = moved_gram(ends, gram, part, chunk)
    rotation_t = pair_rotation(jnp.zeros((1,), jnp.int32), row_parts(gram))
    return last_turn(ends, rotation_t, raw, moved).reshape(col_count, 1, local_rows, WIDTH)


def solution(mesh):
    in_specs = (P(("col", "row"), None), P())
    out_specs = P(None, "row", None, "col")
    return jax.shard_map(local, mesh=mesh, in_specs=in_specs, out_specs=out_specs, check_vma=False)
```

```python
import functools

import jax
import jax.numpy as jnp
from jax import lax
from jax.experimental import pallas as pl
from jax.experimental.pallas import tpu as pltpu
from jax.sharding import PartitionSpec as P

BLOCK = 128
WIDTH = 2 * BLOCK
TILE = 1024
RAW = 1536
CHUNKS = (4608, 2048)
STRIP = 64
PANEL = 32
SUB = 8
HIGHEST = lax.Precision.HIGHEST
COLUMNS = (((0,), (0,)), ((), ()))
LANES = (((1,), (1,)), ((), ()))
F32 = jnp.float32
BF16 = jnp.bfloat16


def grant(megabytes):
    return pltpu.CompilerParams(vmem_limit_bytes=megabytes << 20)


def in_hbm(value):
    return pltpu.with_memory_space_constraint(value, pltpu.HBM)


def two_terms(value):
    high = value.astype(BF16)
    return high, (value - high.astype(F32)).astype(BF16)


def three_terms(value):
    high = value.astype(BF16)
    rest = value - high.astype(F32)
    middle = rest.astype(BF16)
    return high, middle, (rest - middle.astype(F32)).astype(BF16)


def order_kernel(pairing_ref, diffs_ref, out_ref, rows_ref, sems):
    strips = rows_ref.shape[0] // STRIP

    def strip_copy(strip):
        rows = pl.ds(pl.multiple_of(strip * STRIP, STRIP), STRIP)
        return pltpu.make_async_copy(diffs_ref.at[rows, :], rows_ref.at[rows, :], sems.at[strip])

    for strip in range(strips):
        strip_copy(strip).start()

    @pl.loop(0, strips)
    def _(strip):
        strip_copy(strip).wait()
        rows = pl.ds(pl.multiple_of(strip * STRIP, STRIP), STRIP)

        @pl.loop(0, out_ref.shape[0])
        def _(pair):
            for half in range(2):
                column = pl.multiple_of(pairing_ref[2 * pair + half] * BLOCK, BLOCK)
                block = rows_ref[rows, pl.ds(column, BLOCK)]
                out_ref[pair, rows, half * BLOCK : (half + 1) * BLOCK] = block


def order_pairs(diffs, pairing):
    rows, columns = diffs.shape
    return pl.pallas_call(
        order_kernel,
        in_specs=[
            pl.BlockSpec(memory_space=pltpu.SMEM),
            pl.BlockSpec(memory_space=pltpu.HBM),
        ],
        out_specs=pl.BlockSpec(memory_space=pltpu.VMEM),
        out_shape=jax.ShapeDtypeStruct((columns // WIDTH, rows, WIDTH), F32),
        scratch_shapes=[
            pltpu.VMEM((rows, columns), F32),
            pltpu.SemaphoreType.DMA((rows // STRIP,)),
        ],
        compiler_params=grant(24),
        name="order",
    )(pairing, in_hbm(diffs))


def add_gram(tile, total_ref, cross_ref):
    high, low = two_terms(tile)
    total_ref[...] += lax.dot_general(high, high, COLUMNS, preferred_element_type=F32)
    cross_ref[...] += lax.dot_general(high, low, COLUMNS, preferred_element_type=F32)


def for_tiles(rows, body):
    tiles, rest = divmod(rows, TILE)

    @pl.loop(0, tiles)
    def _(tile):
        body(pl.multiple_of(tile * TILE, TILE), TILE, tile)

    if rest:
        body(tiles * TILE, rest, tiles)


def row_copy(source_ref, rows_ref, sems, row, size, tile, start=0):
    source = source_ref.at[pl.ds(pl.multiple_of(row + start, BLOCK), size), :]
    return pltpu.make_async_copy(source, rows_ref.at[pl.ds(row, size), :], sems.at[tile])


def start_rows(source_ref, rows_ref, sems, start=0):
    for tile, row in enumerate(range(0, rows_ref.shape[0], TILE)):
        size = min(TILE, rows_ref.shape[0] - row)
        row_copy(source_ref, rows_ref, sems, row, size, tile, start).start()


def pack(total_ref, cross_ref):
    gram = total_ref[...] + (cross_ref[...] + cross_ref[...].T)
    return jnp.concatenate([gram[:BLOCK, :BLOCK], gram[:BLOCK, BLOCK:], gram[BLOCK:, BLOCK:]])


def unpack(packed):
    corner, side, end = packed[:BLOCK], packed[BLOCK : 2 * BLOCK], packed[2 * BLOCK :]
    upper = jnp.concatenate([corner, side], axis=1)
    return jnp.concatenate([upper, jnp.concatenate([side.T, end], axis=1)])


def gram_kernel(source_ref, out_ref, total_ref, cross_ref, rows_ref, sems):
    start_rows(source_ref, rows_ref, sems)
    total_ref[...] = jnp.zeros_like(total_ref)
    cross_ref[...] = jnp.zeros_like(cross_ref)

    def add(row, size, tile):
        row_copy(source_ref, rows_ref, sems, row, size, tile).wait()
        add_gram(rows_ref[pl.ds(row, size), :], total_ref, cross_ref)

    for_tiles(rows_ref.shape[0], add)
    out_ref[...] = pack(total_ref, cross_ref)


def local_gram(pair_rows):
    rows = pair_rows.shape[0]
    whole = pl.BlockSpec(memory_space=pltpu.VMEM)
    return pl.pallas_call(
        gram_kernel,
        in_specs=[pl.BlockSpec(memory_space=pltpu.HBM)],
        out_specs=whole,
        out_shape=jax.ShapeDtypeStruct((3 * BLOCK, BLOCK), F32),
        scratch_shapes=[
            pltpu.VMEM((WIDTH, WIDTH), F32),
            pltpu.VMEM((WIDTH, WIDTH), F32),
            pltpu.VMEM((rows, WIDTH), F32),
            pltpu.SemaphoreType.DMA((rows // TILE,)),
        ],
        compiler_params=grant(14),
        cost_estimate=pl.CostEstimate(flops=1000, bytes_accessed=1000, transcendentals=0),
        name="gram",
    )(in_hbm(pair_rows))


def cost(rows):
    return pl.CostEstimate(
        flops=6 * rows * WIDTH * WIDTH, bytes_accessed=8 * rows * WIDTH, transcendentals=0
    )


def moved_rows(ends, moved_refs, start, count):
    rows = pl.ds(start, count)
    below, second, above, first = (ref[rows, :] for ref in moved_refs)
    upper = jnp.where(ends[0] == 1, second, below)
    lower = jnp.where(ends[1] == 1, first, above)
    return upper, lower


def moved_tile(ends, moved_refs, row, size):
    return jnp.concatenate(moved_rows(ends, moved_refs, row, size), axis=1)


def moved_gram_kernel(rows, ends, before_ref, *refs):
    moved_refs, (out_ref, total_ref, cross_ref) = refs[:4], refs[4:]
    total_ref[...] = jnp.zeros_like(total_ref)
    cross_ref[...] = jnp.zeros_like(cross_ref)

    def add(row, size, tile):
        add_gram(moved_tile(ends, moved_refs, row, size), total_ref, cross_ref)

    for_tiles(rows, add)

    out_ref[...] = before_ref[...] + pack(total_ref, cross_ref)


def in_vmem(count):
    whole = pl.BlockSpec(memory_space=pltpu.VMEM)
    return [pl.BlockSpec(memory_space=pltpu.SMEM)] + [whole] * count


def moved_gram(ends, before, moved, chunk):
    return pl.pallas_call(
        functools.partial(moved_gram_kernel, chunk),
        in_specs=in_vmem(5),
        out_specs=pl.BlockSpec(memory_space=pltpu.VMEM),
        out_shape=jax.ShapeDtypeStruct((3 * BLOCK, BLOCK), F32),
        scratch_shapes=[pltpu.VMEM((WIDTH, WIDTH), F32)] * 2,
        compiler_params=grant(24),
        cost_estimate=cost(chunk),
        name="moved_gram",
    )(ends, before, *moved)


def row_parts(packed):
    count = lax.axis_size("row")
    step = 1
    while True:
        swap = [(source, source ^ step) for source in range(count)]
        parts = (packed, lax.ppermute(packed, "row", swap))
        step *= 2
        if step >= count:
            return parts
        packed = parts[0] + parts[1]


def outer_product(left, right):
    left1, left2, left3 = three_terms(left)
    right1, right2, right3 = three_terms(right)
    left = jnp.concatenate([left1, left1, left2, left2, left1, left3], axis=0)
    right = jnp.concatenate([right1, right2, right1, right2, right3, right1], axis=0)
    return lax.dot_general(left, right, COLUMNS, preferred_element_type=F32)


def spread(value):
    return jnp.broadcast_to(value, (SUB, BLOCK))


def total(terms):
    while len(terms) > 1:
        paired = [a + b for a, b in zip(terms[::2], terms[1::2])]
        terms = paired + terms[len(terms) - len(terms) % 2 :]
    return terms[0]


def small_inverse(tile, lane, spread_ref, base):
    for j in range(SUB):
        spread_ref[base + SUB * j : base + SUB * (j + 1), :] = spread(tile[:, lane + j : lane + j + 1])
    entry = {
        (i, j): spread_ref[pl.ds(base + SUB * j + i, SUB, stride=0), :]
        for j in range(SUB)
        for i in range(j, SUB)
    }
    lower, scales = {}, []
    for j in range(SUB):
        scale = lax.rsqrt(entry[j, j])
        inverse = scale * scale
        scales.append(scale)
        for i in range(j + 1, SUB):
            lower[i, j] = entry[i, j] * inverse
        for m in range(j + 1, SUB):
            for i in range(m, SUB):
                entry[i, m] = entry[i, m] - lower[i, j] * entry[m, j]
    solved = {}
    for j in range(SUB):
        for i in range(j + 1, SUB):
            terms = [lower[i, j]] + [lower[i, m] * solved[m, j] for m in range(j + 1, i)]
            solved[i, j] = -total(terms)
    solved = {at: value * scales[at[0]] for at, value in solved.items()}
    return solved | {(j, j): scales[j] for j in range(SUB)}


def tiles_of(ref, start, end, first, last):
    return jnp.concatenate([ref[t, start:end, :] for t in range(first, last)], axis=1)


def put_tiles(ref, first, value):
    for t in range(value.shape[1] // BLOCK):
        ref[first + t] = value[:, BLOCK * t : BLOCK * (t + 1)]


def eliminate(work_ref, factor_ref, spread_ref, tiles):
    row = lax.broadcasted_iota(jnp.int32, (SUB, BLOCK), 0)
    lane = lax.broadcasted_iota(jnp.int32, (SUB, BLOCK), 1)
    zero = jnp.zeros((SUB, BLOCK), F32)
    for start in range(0, WIDTH, PANEL):
        end = start + PANEL
        own = start // BLOCK
        for top in range(start, end, SUB):
            at = top % BLOCK
            base = SUB * SUB * (top // SUB % 2)
            small = small_inverse(work_ref[own, top : top + SUB, :], at, spread_ref, base)
            columns = []
            for j in range(SUB):
                column = zero
                for i in range(j, SUB):
                    column = jnp.where(row == i, small[i, j], column)
                columns.append(column)
            for t in range(tiles):
                if t < own:
                    solved = zero
                else:
                    solved = total(
                        [columns[j] * work_ref[t, pl.ds(top + j, SUB, stride=0), :] for j in range(SUB)]
                    )
                    if t == own:
                        solved = jnp.where(lane >= row + at, solved, 0.0)
                factor_ref[t, top : top + SUB, :] = solved
            for below in range(top + SUB, end, SUB):
                tile = work_ref[own, below : below + SUB, :]
                entries = [spread(tile[:, at + j : at + j + 1]) for j in range(SUB)]
                left = [total([entries[j] * small[i, j] for j in range(i + 1)]) for i in range(SUB)]
                for t in range(own, tiles):
                    work_ref[t, below : below + SUB, :] -= total(
                        [left[i] * factor_ref[t, pl.ds(top + i, SUB, stride=0), :] for i in range(SUB)]
                    )
        if end < WIDTH:
            first = end // BLOCK
            update = outer_product(
                tiles_of(factor_ref, start, end, first, WIDTH // BLOCK),
                tiles_of(factor_ref, start, end, first, tiles),
            )
            for t in range(first, tiles):
                here = BLOCK * (t - first)
                work_ref[t, end:, :] -= update[end - BLOCK * first :, here : here + BLOCK]


def rotation_kernel(swap_ref, one_ref, two_ref, first_ref, second_ref, work_ref, factor_ref, spread_ref):
    gram = unpack(one_ref[...] + two_ref[...])
    square = jnp.dot(gram, gram, precision=HIGHEST, preferred_element_type=F32)
    put_tiles(work_ref, 0, square)
    eliminate(work_ref, factor_ref, spread_ref, WIDTH // BLOCK)
    factor = tiles_of(factor_ref, 0, WIDTH, 0, WIDTH // BLOCK)
    square = lax.dot_general(factor, factor, LANES, precision=HIGHEST, preferred_element_type=F32)
    put_tiles(work_ref, 0, square)
    put_tiles(work_ref, WIDTH // BLOCK, factor)
    eliminate(work_ref, factor_ref, spread_ref, 2 * WIDTH // BLOCK)
    halves = [
        tiles_of(factor_ref, start, start + BLOCK, WIDTH // BLOCK, 2 * WIDTH // BLOCK)
        for start in (0, BLOCK)
    ]
    first_ref[...] = jnp.where(swap_ref[0] == 1, halves[1], halves[0])
    second_ref[...] = jnp.where(swap_ref[0] == 1, halves[0], halves[1])


def pair_rotation(swap, parts):
    tiles = pltpu.VMEM((2 * WIDTH // BLOCK, WIDTH, BLOCK), F32)
    return pl.pallas_call(
        rotation_kernel,
        in_specs=[pl.BlockSpec(memory_space=pltpu.SMEM)] + [pl.BlockSpec(memory_space=pltpu.VMEM)] * 2,
        out_shape=[jax.ShapeDtypeStruct((BLOCK, WIDTH), F32)] * 2,
        scratch_shapes=[tiles, tiles, pltpu.VMEM((2 * SUB * SUB, BLOCK), F32)],
        compiler_params=grant(8),
        cost_estimate=pl.CostEstimate(flops=1000, bytes_accessed=1000, transcendentals=0),
        name="rotation",
    )(swap, *parts)


def product(rows, rotation_t):
    high, low = two_terms(rows)
    turn_high, turn_low = two_terms(rotation_t)
    turned = lax.dot_general(high, turn_high, LANES, preferred_element_type=F32)
    turned += lax.dot_general(low, turn_high, LANES, preferred_element_type=F32)
    return turned + lax.dot_general(high, turn_low, LANES, preferred_element_type=F32)


def turn_kernel(start, source_ref, one_ref, two_ref, first_ref, second_ref, rows_ref, sems):
    start_rows(source_ref, rows_ref, sems, start)
    rotation_t = jnp.concatenate([one_ref[...], two_ref[...]])
    if first_ref.shape[0] > rows_ref.shape[0]:
        for half_ref, out_ref in ((one_ref, first_ref), (two_ref, second_ref)):
            end = rows_ref.shape[0]
            out_ref[end : end + BLOCK, :] = half_ref[:, :BLOCK]
            out_ref[end + BLOCK :, :] = half_ref[:, BLOCK:]

    def put(row, size, tile):
        row_copy(source_ref, rows_ref, sems, row, size, tile, start).wait()
        rows = pl.ds(row, size)
        turned = product(rows_ref[rows, :], rotation_t)
        first_ref[rows, :] = turned[:, :BLOCK]
        second_ref[rows, :] = turned[:, BLOCK:]

    for_tiles(rows_ref.shape[0], put)


def turn(pair_rows, rotation_t, start, rows, extra):
    whole = pl.BlockSpec(memory_space=pltpu.VMEM)
    return pl.pallas_call(
        functools.partial(turn_kernel, start),
        in_specs=[pl.BlockSpec(memory_space=pltpu.HBM), whole, whole],
        out_specs=[whole, whole],
        out_shape=[jax.ShapeDtypeStruct((rows + extra, BLOCK), F32)] * 2,
        scratch_shapes=[
            pltpu.VMEM((rows, WIDTH), F32),
            pltpu.SemaphoreType.DMA((pl.cdiv(rows, TILE),)),
        ],
        compiler_params=grant(24),
        cost_estimate=cost(rows if extra else 30 * rows),
        name="turn",
    )(in_hbm(pair_rows), *rotation_t)


def raw_gram_kernel(ends, below_ref, above_ref, own_ref, *refs):
    moved_refs, (out_ref, packed_ref, total_ref, cross_ref) = refs[:4], refs[4:]
    total_ref[...] = jnp.zeros_like(total_ref)
    cross_ref[...] = jnp.zeros_like(cross_ref)
    halves_t = [
        jnp.concatenate([half[:BLOCK], half[BLOCK:]], axis=1)
        for half in moved_rows(ends, moved_refs, CHUNKS[0], WIDTH)
    ]

    def put(row, size, tile):
        rows = pl.ds(row, size)
        own = own_ref[rows, :]
        upper = product(jnp.where(ends[0] == 1, own, below_ref[rows, :]), halves_t[0])
        lower = product(jnp.where(ends[1] == 1, own, above_ref[rows, :]), halves_t[1])
        turned = jnp.concatenate([upper, lower], axis=1)
        out_ref[rows, :] = turned
        add_gram(turned, total_ref, cross_ref)

    for_tiles(RAW, put)
    packed_ref[...] = pack(total_ref, cross_ref)


def raw_gram(ends, below, above, own, moved):
    whole = pl.BlockSpec(memory_space=pltpu.VMEM)
    return pl.pallas_call(
        raw_gram_kernel,
        in_specs=in_vmem(7),
        out_specs=[whole, whole],
        out_shape=[
            jax.ShapeDtypeStruct((RAW, WIDTH), F32),
            jax.ShapeDtypeStruct((3 * BLOCK, BLOCK), F32),
        ],
        scratch_shapes=[pltpu.VMEM((WIDTH, WIDTH), F32)] * 2,
        compiler_params=grant(24),
        cost_estimate=cost(2 * RAW),
        name="raw_gram",
    )(ends, below, above, own, *moved)


def last_turn_kernel(ends, one_ref, two_ref, raw_ref, *refs):
    moved, (out_ref, turned_ref, sems) = (refs[0:4], refs[4:8]), refs[8:]
    rotation_t = jnp.concatenate([one_ref[...], two_ref[...]])

    def out_copy(row, size, sem):
        rows = pl.ds(pl.multiple_of(row, BLOCK), size)
        return pltpu.make_async_copy(turned_ref.at[rows, :], out_ref.at[rows, :], sems.at[sem])

    start, sem = 0, 0
    copies = []
    for moved_refs, count in zip((None, *moved), (RAW, *CHUNKS)):

        def put(row, size, tile, moved_refs=moved_refs, start=start, sem=sem):
            if moved_refs is None:
                rows = raw_ref[pl.ds(row, size), :]
            else:
                rows = moved_tile(ends, moved_refs, row, size)
            at = pl.ds(pl.multiple_of(start + row, BLOCK), size)
            turned_ref[at, :] = product(rows, rotation_t)
            out_copy(start + row, size, sem + tile).start()

        for_tiles(count, put)
        for row in range(0, count, TILE):
            copies.append((start + row, min(TILE, count - row), sem))
            sem += 1
        start += count
    for copy in copies:
        out_copy(*copy).wait()


def last_turn(ends, rotation_t, raw, moved):
    rows = RAW + sum(CHUNKS)
    tiles = sum(pl.cdiv(count, TILE) for count in (RAW, *CHUNKS))
    moved = [array for part in moved for array in part]
    return pl.pallas_call(
        last_turn_kernel,
        in_specs=in_vmem(3 + len(moved)),
        out_specs=pl.BlockSpec(memory_space=pl.ANY),
        out_shape=jax.ShapeDtypeStruct((rows, WIDTH), F32),
        scratch_shapes=[
            pltpu.VMEM((rows, WIDTH), F32),
            pltpu.SemaphoreType.DMA((tiles,)),
        ],
        compiler_params=grant(24),
        cost_estimate=cost(rows),
        name="last_turn",
    )(ends, *rotation_t, raw, *moved)


def send_up(value):
    count = lax.axis_size("col")
    return lax.ppermute(value, "col", [(p, p + 1) for p in range(count - 1)])


def send_down(value):
    count = lax.axis_size("col")
    return lax.ppermute(value, "col", [(p, p - 1) for p in range(1, count)])


def local(diffs, pairing):
    col_count = lax.axis_size("col")
    position = lax.axis_index("col")
    local_rows = diffs.shape[0]
    rows = col_count * local_rows
    bottom, top = position == 0, position == col_count - 1
    ends = jnp.stack([bottom, top]).astype(jnp.int32)
    ordered = order_pairs(diffs, pairing)
    pair_rows = lax.all_to_all(ordered, "col", split_axis=0, concat_axis=0, tiled=True)
    pair_rows = pair_rows.reshape(rows, WIDTH)

    parts = row_parts(local_gram(pair_rows))
    *parts, own = lax.optimization_barrier((*parts, pair_rows[:RAW]))
    below, above = send_up(own), send_down(own)
    rotation_t = pair_rotation(ends[:1], parts)
    moved, start = [], RAW
    for number, chunk in enumerate(CHUNKS):
        first, second = turn(pair_rows, rotation_t, start, chunk, 0 if number else WIDTH)
        if number == 1:
            first, second, below, above = lax.optimization_barrier((first, second, below, above))
        moved.append((send_up(first), second, send_down(second), first))
        start += chunk
    raw, gram = raw_gram(ends, below, above, own, moved[0])
    for part, chunk in zip(moved, CHUNKS):
        gram = moved_gram(ends, gram, part, chunk)
    rotation_t = pair_rotation(jnp.zeros((1,), jnp.int32), row_parts(gram))
    return last_turn(ends, rotation_t, raw, moved).reshape(col_count, 1, local_rows, WIDTH)


def solution(mesh):
    in_specs = (P(("col", "row"), None), P())
    out_specs = P(None, "row", None, "col")
    return jax.shard_map(local, mesh=mesh, in_specs=in_specs, out_specs=out_specs, check_vma=False)
```

```python
import functools

import jax
import jax.numpy as jnp
from jax import lax
from jax.experimental import pallas as pl
from jax.experimental.pallas import tpu as pltpu
from jax.sharding import PartitionSpec as P

BLOCK = 128
WIDTH = 2 * BLOCK
TILE = 1024
CHUNKS = (3072, 3072, 2048)
STRIP = 64
PANEL = 32
SUB = 8
HIGHEST = lax.Precision.HIGHEST
COLUMNS = (((0,), (0,)), ((), ()))
LANES = (((1,), (1,)), ((), ()))
F32 = jnp.float32
BF16 = jnp.bfloat16


def grant(megabytes):
    return pltpu.CompilerParams(vmem_limit_bytes=megabytes << 20)


def in_hbm(value):
    return pltpu.with_memory_space_constraint(value, pltpu.HBM)


def two_terms(value):
    high = value.astype(BF16)
    return high, (value - high.astype(F32)).astype(BF16)


def three_terms(value):
    high = value.astype(BF16)
    rest = value - high.astype(F32)
    middle = rest.astype(BF16)
    return high, middle, (rest - middle.astype(F32)).astype(BF16)


def order_kernel(pairing_ref, diffs_ref, out_ref, rows_ref, sems):
    strips = rows_ref.shape[0] // STRIP

    def strip_copy(strip):
        rows = pl.ds(pl.multiple_of(strip * STRIP, STRIP), STRIP)
        return pltpu.make_async_copy(diffs_ref.at[rows, :], rows_ref.at[rows, :], sems.at[strip])

    for strip in range(strips):
        strip_copy(strip).start()

    @pl.loop(0, strips)
    def _(strip):
        strip_copy(strip).wait()
        rows = pl.ds(pl.multiple_of(strip * STRIP, STRIP), STRIP)

        @pl.loop(0, out_ref.shape[0])
        def _(pair):
            for half in range(2):
                column = pl.multiple_of(pairing_ref[2 * pair + half] * BLOCK, BLOCK)
                block = rows_ref[rows, pl.ds(column, BLOCK)]
                out_ref[pair, rows, half * BLOCK : (half + 1) * BLOCK] = block


def order_pairs(diffs, pairing):
    rows, columns = diffs.shape
    return pl.pallas_call(
        order_kernel,
        in_specs=[
            pl.BlockSpec(memory_space=pltpu.SMEM),
            pl.BlockSpec(memory_space=pltpu.HBM),
        ],
        out_specs=pl.BlockSpec(memory_space=pltpu.VMEM),
        out_shape=jax.ShapeDtypeStruct((columns // WIDTH, rows, WIDTH), F32),
        scratch_shapes=[
            pltpu.VMEM((rows, columns), F32),
            pltpu.SemaphoreType.DMA((rows // STRIP,)),
        ],
        compiler_params=grant(24),
        name="order",
    )(pairing, in_hbm(diffs))


def add_gram(tile, total_ref, cross_ref):
    high, low = two_terms(tile)
    total_ref[...] += lax.dot_general(high, high, COLUMNS, preferred_element_type=F32)
    cross_ref[...] += lax.dot_general(high, low, COLUMNS, preferred_element_type=F32)


def for_tiles(rows, body):
    tiles, rest = divmod(rows, TILE)

    @pl.loop(0, tiles)
    def _(tile):
        body(pl.multiple_of(tile * TILE, TILE), TILE, tile)

    if rest:
        body(tiles * TILE, rest, tiles)


def row_copy(source_ref, rows_ref, sems, row, size, tile, start=0):
    source = source_ref.at[pl.ds(pl.multiple_of(row + start, BLOCK), size), :]
    return pltpu.make_async_copy(source, rows_ref.at[pl.ds(row, size), :], sems.at[tile])


def start_rows(source_ref, rows_ref, sems, start=0):
    for tile, row in enumerate(range(0, rows_ref.shape[0], TILE)):
        size = min(TILE, rows_ref.shape[0] - row)
        row_copy(source_ref, rows_ref, sems, row, size, tile, start).start()


def pack(total_ref, cross_ref):
    gram = total_ref[...] + (cross_ref[...] + cross_ref[...].T)
    return jnp.concatenate([gram[:BLOCK, :BLOCK], gram[:BLOCK, BLOCK:], gram[BLOCK:, BLOCK:]])


def unpack(packed):
    corner, side, end = packed[:BLOCK], packed[BLOCK : 2 * BLOCK], packed[2 * BLOCK :]
    upper = jnp.concatenate([corner, side], axis=1)
    return jnp.concatenate([upper, jnp.concatenate([side.T, end], axis=1)])


def gram_kernel(source_ref, out_ref, total_ref, cross_ref, rows_ref, sems):
    start_rows(source_ref, rows_ref, sems)
    total_ref[...] = jnp.zeros_like(total_ref)
    cross_ref[...] = jnp.zeros_like(cross_ref)

    def add(row, size, tile):
        row_copy(source_ref, rows_ref, sems, row, size, tile).wait()
        add_gram(rows_ref[pl.ds(row, size), :], total_ref, cross_ref)

    for_tiles(rows_ref.shape[0], add)
    out_ref[...] = pack(total_ref, cross_ref)


def local_gram(pair_rows):
    rows = pair_rows.shape[0]
    whole = pl.BlockSpec(memory_space=pltpu.VMEM)
    return pl.pallas_call(
        gram_kernel,
        in_specs=[pl.BlockSpec(memory_space=pltpu.HBM)],
        out_specs=whole,
        out_shape=jax.ShapeDtypeStruct((3 * BLOCK, BLOCK), F32),
        scratch_shapes=[
            pltpu.VMEM((WIDTH, WIDTH), F32),
            pltpu.VMEM((WIDTH, WIDTH), F32),
            pltpu.VMEM((rows, WIDTH), F32),
            pltpu.SemaphoreType.DMA((rows // TILE,)),
        ],
        compiler_params=grant(14),
        cost_estimate=pl.CostEstimate(flops=1000, bytes_accessed=1000, transcendentals=0),
        name="gram",
    )(in_hbm(pair_rows))


def cost(rows):
    return pl.CostEstimate(
        flops=6 * rows * WIDTH * WIDTH, bytes_accessed=8 * rows * WIDTH, transcendentals=0
    )


def moved_rows(ends, moved_refs, start, count):
    rows = pl.ds(start, count)
    below, second, above, first = (ref[rows, :] for ref in moved_refs)
    upper = jnp.where(ends[0] == 1, second, below)
    lower = jnp.where(ends[1] == 1, first, above)
    return upper, lower


def moved_tile(ends, moved_refs, row, size):
    return jnp.concatenate(moved_rows(ends, moved_refs, row, size), axis=1)


def moved_gram_kernel(rows, ends, before_ref, *refs):
    moved_refs, (out_ref, total_ref, cross_ref) = refs[:4], refs[4:]
    total_ref[...] = jnp.zeros_like(total_ref)
    cross_ref[...] = jnp.zeros_like(cross_ref)

    def add(row, size, tile):
        add_gram(moved_tile(ends, moved_refs, row, size), total_ref, cross_ref)

    for_tiles(rows, add)

    out_ref[...] = before_ref[...] + pack(total_ref, cross_ref)


def in_vmem(count):
    whole = pl.BlockSpec(memory_space=pltpu.VMEM)
    return [pl.BlockSpec(memory_space=pltpu.SMEM)] + [whole] * count


def moved_gram(ends, before, moved, chunk):
    return pl.pallas_call(
        functools.partial(moved_gram_kernel, chunk),
        in_specs=in_vmem(5),
        out_specs=pl.BlockSpec(memory_space=pltpu.VMEM),
        out_shape=jax.ShapeDtypeStruct((3 * BLOCK, BLOCK), F32),
        scratch_shapes=[pltpu.VMEM((WIDTH, WIDTH), F32)] * 2,
        compiler_params=grant(24),
        cost_estimate=cost(chunk),
        name="moved_gram",
    )(ends, before, *moved)


def row_parts(packed):
    count = lax.axis_size("row")
    step = 1
    while True:
        swap = [(source, source ^ step) for source in range(count)]
        parts = (packed, lax.ppermute(packed, "row", swap))
        step *= 2
        if step >= count:
            return parts
        packed = parts[0] + parts[1]


def outer_product(left, right):
    left1, left2, left3 = three_terms(left)
    right1, right2, right3 = three_terms(right)
    left = jnp.concatenate([left1, left1, left2, left2, left1, left3], axis=0)
    right = jnp.concatenate([right1, right2, right1, right2, right3, right1], axis=0)
    return lax.dot_general(left, right, COLUMNS, preferred_element_type=F32)


def spread(value):
    return jnp.broadcast_to(value, (SUB, BLOCK))


def total(terms):
    while len(terms) > 1:
        paired = [a + b for a, b in zip(terms[::2], terms[1::2])]
        terms = paired + terms[len(terms) - len(terms) % 2 :]
    return terms[0]


def small_inverse(tile, lane, spread_ref, base):
    for j in range(SUB):
        spread_ref[base + SUB * j : base + SUB * (j + 1), :] = spread(tile[:, lane + j : lane + j + 1])
    entry = {
        (i, j): spread_ref[pl.ds(base + SUB * j + i, SUB, stride=0), :]
        for j in range(SUB)
        for i in range(j, SUB)
    }
    lower, scales = {}, []
    for j in range(SUB):
        scale = lax.rsqrt(entry[j, j])
        inverse = scale * scale
        scales.append(scale)
        for i in range(j + 1, SUB):
            lower[i, j] = entry[i, j] * inverse
        for m in range(j + 1, SUB):
            for i in range(m, SUB):
                entry[i, m] = entry[i, m] - lower[i, j] * entry[m, j]
    solved = {}
    for j in range(SUB):
        for i in range(j + 1, SUB):
            terms = [lower[i, j]] + [lower[i, m] * solved[m, j] for m in range(j + 1, i)]
            solved[i, j] = -total(terms)
    solved = {at: value * scales[at[0]] for at, value in solved.items()}
    return solved | {(j, j): scales[j] for j in range(SUB)}


def tiles_of(ref, start, end, first, last):
    return jnp.concatenate([ref[t, start:end, :] for t in range(first, last)], axis=1)


def put_tiles(ref, first, value):
    for t in range(value.shape[1] // BLOCK):
        ref[first + t] = value[:, BLOCK * t : BLOCK * (t + 1)]


def eliminate(work_ref, factor_ref, spread_ref, tiles):
    row = lax.broadcasted_iota(jnp.int32, (SUB, BLOCK), 0)
    lane = lax.broadcasted_iota(jnp.int32, (SUB, BLOCK), 1)
    zero = jnp.zeros((SUB, BLOCK), F32)
    for start in range(0, WIDTH, PANEL):
        end = start + PANEL
        own = start // BLOCK
        for top in range(start, end, SUB):
            at = top % BLOCK
            base = SUB * SUB * (top // SUB % 2)
            small = small_inverse(work_ref[own, top : top + SUB, :], at, spread_ref, base)
            columns = []
            for j in range(SUB):
                column = zero
                for i in range(j, SUB):
                    column = jnp.where(row == i, small[i, j], column)
                columns.append(column)
            for t in range(tiles):
                if t < own:
                    solved = zero
                else:
                    solved = total(
                        [columns[j] * work_ref[t, pl.ds(top + j, SUB, stride=0), :] for j in range(SUB)]
                    )
                    if t == own:
                        solved = jnp.where(lane >= row + at, solved, 0.0)
                factor_ref[t, top : top + SUB, :] = solved
            for below in range(top + SUB, end, SUB):
                tile = work_ref[own, below : below + SUB, :]
                entries = [spread(tile[:, at + j : at + j + 1]) for j in range(SUB)]
                left = [total([entries[j] * small[i, j] for j in range(i + 1)]) for i in range(SUB)]
                for t in range(own, tiles):
                    work_ref[t, below : below + SUB, :] -= total(
                        [left[i] * factor_ref[t, pl.ds(top + i, SUB, stride=0), :] for i in range(SUB)]
                    )
        if end < WIDTH:
            first = end // BLOCK
            update = outer_product(
                tiles_of(factor_ref, start, end, first, WIDTH // BLOCK),
                tiles_of(factor_ref, start, end, first, tiles),
            )
            for t in range(first, tiles):
                here = BLOCK * (t - first)
                work_ref[t, end:, :] -= update[end - BLOCK * first :, here : here + BLOCK]


def rotation_kernel(swap_ref, one_ref, two_ref, first_ref, second_ref, work_ref, factor_ref, spread_ref):
    gram = unpack(one_ref[...] + two_ref[...])
    square = jnp.dot(gram, gram, precision=HIGHEST, preferred_element_type=F32)
    put_tiles(work_ref, 0, square)
    eliminate(work_ref, factor_ref, spread_ref, WIDTH // BLOCK)
    factor = tiles_of(factor_ref, 0, WIDTH, 0, WIDTH // BLOCK)
    square = lax.dot_general(factor, factor, LANES, precision=HIGHEST, preferred_element_type=F32)
    put_tiles(work_ref, 0, square)
    put_tiles(work_ref, WIDTH // BLOCK, factor)
    eliminate(work_ref, factor_ref, spread_ref, 2 * WIDTH // BLOCK)
    halves = [
        tiles_of(factor_ref, start, start + BLOCK, WIDTH // BLOCK, 2 * WIDTH // BLOCK)
        for start in (0, BLOCK)
    ]
    first_ref[...] = jnp.where(swap_ref[0] == 1, halves[1], halves[0])
    second_ref[...] = jnp.where(swap_ref[0] == 1, halves[0], halves[1])


def pair_rotation(swap, parts):
    tiles = pltpu.VMEM((2 * WIDTH // BLOCK, WIDTH, BLOCK), F32)
    return pl.pallas_call(
        rotation_kernel,
        in_specs=[pl.BlockSpec(memory_space=pltpu.SMEM)] + [pl.BlockSpec(memory_space=pltpu.VMEM)] * 2,
        out_shape=[jax.ShapeDtypeStruct((BLOCK, WIDTH), F32)] * 2,
        scratch_shapes=[tiles, tiles, pltpu.VMEM((2 * SUB * SUB, BLOCK), F32)],
        compiler_params=grant(8),
        cost_estimate=pl.CostEstimate(flops=1000, bytes_accessed=1000, transcendentals=0),
        name="rotation",
    )(swap, *parts)


def product(rows, rotation_t):
    high, low = two_terms(rows)
    turn_high, turn_low = two_terms(rotation_t)
    turned = lax.dot_general(high, turn_high, LANES, preferred_element_type=F32)
    turned += lax.dot_general(low, turn_high, LANES, preferred_element_type=F32)
    return turned + lax.dot_general(high, turn_low, LANES, preferred_element_type=F32)


def turn_kernel(start, source_ref, one_ref, two_ref, first_ref, second_ref, rows_ref, sems):
    start_rows(source_ref, rows_ref, sems, start)
    rotation_t = jnp.concatenate([one_ref[...], two_ref[...]])

    def put(row, size, tile):
        row_copy(source_ref, rows_ref, sems, row, size, tile, start).wait()
        rows = pl.ds(row, size)
        turned = product(rows_ref[rows, :], rotation_t)
        first_ref[rows, :] = turned[:, :BLOCK]
        second_ref[rows, :] = turned[:, BLOCK:]

    for_tiles(rows_ref.shape[0], put)


def turn(pair_rows, rotation_t, start, rows):
    whole = pl.BlockSpec(memory_space=pltpu.VMEM)
    return pl.pallas_call(
        functools.partial(turn_kernel, start),
        in_specs=[pl.BlockSpec(memory_space=pltpu.HBM), whole, whole],
        out_specs=[whole, whole],
        out_shape=[jax.ShapeDtypeStruct((rows, BLOCK), F32)] * 2,
        scratch_shapes=[
            pltpu.VMEM((rows, WIDTH), F32),
            pltpu.SemaphoreType.DMA((pl.cdiv(rows, TILE),)),
        ],
        compiler_params=grant(24),
        cost_estimate=cost(rows),
        name="turn",
    )(in_hbm(pair_rows), *rotation_t)


def last_turn_kernel(ends, one_ref, two_ref, *refs):
    arrays = 4 * len(CHUNKS)
    moved = [refs[at : at + 4] for at in range(0, arrays, 4)]
    out_ref, turned_ref, sems = refs[arrays:]
    rotation_t = jnp.concatenate([one_ref[...], two_ref[...]])

    def out_copy(row, size, sem):
        rows = pl.ds(pl.multiple_of(row, BLOCK), size)
        return pltpu.make_async_copy(turned_ref.at[rows, :], out_ref.at[rows, :], sems.at[sem])

    start, sem = 0, 0
    copies = []
    for moved_refs, count in zip(moved, CHUNKS):

        def put(row, size, tile, moved_refs=moved_refs, start=start, sem=sem):
            rows = moved_tile(ends, moved_refs, row, size)
            at = pl.ds(pl.multiple_of(start + row, BLOCK), size)
            turned_ref[at, :] = product(rows, rotation_t)
            out_copy(start + row, size, sem + tile).start()

        for_tiles(count, put)
        for row in range(0, count, TILE):
            copies.append((start + row, min(TILE, count - row), sem))
            sem += 1
        start += count
    for copy in copies:
        out_copy(*copy).wait()


def last_turn(ends, rotation_t, moved):
    rows = sum(CHUNKS)
    tiles = sum(pl.cdiv(count, TILE) for count in CHUNKS)
    moved = [array for part in moved for array in part]
    return pl.pallas_call(
        last_turn_kernel,
        in_specs=in_vmem(2 + len(moved)),
        out_specs=pl.BlockSpec(memory_space=pl.ANY),
        out_shape=jax.ShapeDtypeStruct((rows, WIDTH), F32),
        scratch_shapes=[
            pltpu.VMEM((rows, WIDTH), F32),
            pltpu.SemaphoreType.DMA((tiles,)),
        ],
        compiler_params=grant(24),
        cost_estimate=cost(rows),
        name="last_turn",
    )(ends, *rotation_t, *moved)


def send_up(value):
    count = lax.axis_size("col")
    return lax.ppermute(value, "col", [(p, p + 1) for p in range(count - 1)])


def send_down(value):
    count = lax.axis_size("col")
    return lax.ppermute(value, "col", [(p, p - 1) for p in range(1, count)])


def local(diffs, pairing):
    col_count = lax.axis_size("col")
    position = lax.axis_index("col")
    local_rows = diffs.shape[0]
    rows = col_count * local_rows
    bottom, top = position == 0, position == col_count - 1
    ends = jnp.stack([bottom, top]).astype(jnp.int32)
    ordered = order_pairs(diffs, pairing)
    pair_rows = lax.all_to_all(ordered, "col", split_axis=0, concat_axis=0, tiled=True)
    pair_rows = pair_rows.reshape(rows, WIDTH)

    rotation_t = pair_rotation(ends[:1], row_parts(local_gram(pair_rows)))
    moved, start = [], 0
    for chunk in CHUNKS:
        first, second = turn(pair_rows, rotation_t, start, chunk)
        moved.append((send_up(first), second, send_down(second), first))
        start += chunk
    gram = jnp.zeros((3 * BLOCK, BLOCK), F32)
    for part, chunk in zip(moved, CHUNKS):
        gram = moved_gram(ends, gram, part, chunk)
    rotation_t = pair_rotation(jnp.zeros((1,), jnp.int32), row_parts(gram))
    return last_turn(ends, rotation_t, moved).reshape(col_count, 1, local_rows, WIDTH)


def solution(mesh):
    in_specs = (P(("col", "row"), None), P())
    out_specs = P(None, "row", None, "col")
    return jax.shard_map(local, mesh=mesh, in_specs=in_specs, out_specs=out_specs, check_vma=False)
```

```python
import functools

import jax
import jax.numpy as jnp
from jax import lax
from jax.experimental import pallas as pl
from jax.experimental.pallas import tpu as pltpu
from jax.sharding import PartitionSpec as P

BLOCK = 128
WIDTH = 2 * BLOCK
TILE = 1024
CHUNKS = (3584, 3584, 1024)
STRIP = 64
PANEL = 32
SUB = 8
HIGHEST = lax.Precision.HIGHEST
COLUMNS = (((0,), (0,)), ((), ()))
LANES = (((1,), (1,)), ((), ()))
F32 = jnp.float32
BF16 = jnp.bfloat16


def grant(megabytes):
    return pltpu.CompilerParams(vmem_limit_bytes=megabytes << 20)


def in_hbm(value):
    return pltpu.with_memory_space_constraint(value, pltpu.HBM)


def two_terms(value):
    high = value.astype(BF16)
    return high, (value - high.astype(F32)).astype(BF16)


def three_terms(value):
    high = value.astype(BF16)
    rest = value - high.astype(F32)
    middle = rest.astype(BF16)
    return high, middle, (rest - middle.astype(F32)).astype(BF16)


def order_kernel(pairing_ref, diffs_ref, out_ref, rows_ref, sems):
    strips = rows_ref.shape[0] // STRIP

    def strip_copy(strip):
        rows = pl.ds(pl.multiple_of(strip * STRIP, STRIP), STRIP)
        return pltpu.make_async_copy(diffs_ref.at[rows, :], rows_ref.at[rows, :], sems.at[strip])

    for strip in range(strips):
        strip_copy(strip).start()

    @pl.loop(0, strips)
    def _(strip):
        strip_copy(strip).wait()
        rows = pl.ds(pl.multiple_of(strip * STRIP, STRIP), STRIP)

        @pl.loop(0, out_ref.shape[0])
        def _(pair):
            for half in range(2):
                column = pl.multiple_of(pairing_ref[2 * pair + half] * BLOCK, BLOCK)
                block = rows_ref[rows, pl.ds(column, BLOCK)]
                out_ref[pair, rows, half * BLOCK : (half + 1) * BLOCK] = block


def order_pairs(diffs, pairing):
    rows, columns = diffs.shape
    return pl.pallas_call(
        order_kernel,
        in_specs=[
            pl.BlockSpec(memory_space=pltpu.SMEM),
            pl.BlockSpec(memory_space=pltpu.HBM),
        ],
        out_specs=pl.BlockSpec(memory_space=pltpu.VMEM),
        out_shape=jax.ShapeDtypeStruct((columns // WIDTH, rows, WIDTH), F32),
        scratch_shapes=[
            pltpu.VMEM((rows, columns), F32),
            pltpu.SemaphoreType.DMA((rows // STRIP,)),
        ],
        compiler_params=grant(24),
        name="order",
    )(pairing, in_hbm(diffs))


def add_gram(tile, total_ref, cross_ref):
    high, low = two_terms(tile)
    total_ref[...] += lax.dot_general(high, high, COLUMNS, preferred_element_type=F32)
    cross_ref[...] += lax.dot_general(high, low, COLUMNS, preferred_element_type=F32)


def for_tiles(rows, body):
    tiles, rest = divmod(rows, TILE)

    @pl.loop(0, tiles)
    def _(tile):
        body(pl.multiple_of(tile * TILE, TILE), TILE, tile)

    if rest:
        body(tiles * TILE, rest, tiles)


def row_copy(source_ref, rows_ref, sems, row, size, tile, start=0):
    source = source_ref.at[pl.ds(pl.multiple_of(row + start, BLOCK), size), :]
    return pltpu.make_async_copy(source, rows_ref.at[pl.ds(row, size), :], sems.at[tile])


def start_rows(source_ref, rows_ref, sems, start=0):
    for tile, row in enumerate(range(0, rows_ref.shape[0], TILE)):
        size = min(TILE, rows_ref.shape[0] - row)
        row_copy(source_ref, rows_ref, sems, row, size, tile, start).start()


def pack(total_ref, cross_ref):
    gram = total_ref[...] + (cross_ref[...] + cross_ref[...].T)
    return jnp.concatenate([gram[:BLOCK, :BLOCK], gram[:BLOCK, BLOCK:], gram[BLOCK:, BLOCK:]])


def unpack(packed):
    corner, side, end = packed[:BLOCK], packed[BLOCK : 2 * BLOCK], packed[2 * BLOCK :]
    upper = jnp.concatenate([corner, side], axis=1)
    return jnp.concatenate([upper, jnp.concatenate([side.T, end], axis=1)])


def gram_kernel(source_ref, out_ref, total_ref, cross_ref, rows_ref, sems):
    start_rows(source_ref, rows_ref, sems)
    total_ref[...] = jnp.zeros_like(total_ref)
    cross_ref[...] = jnp.zeros_like(cross_ref)

    def add(row, size, tile):
        row_copy(source_ref, rows_ref, sems, row, size, tile).wait()
        add_gram(rows_ref[pl.ds(row, size), :], total_ref, cross_ref)

    for_tiles(rows_ref.shape[0], add)
    out_ref[...] = pack(total_ref, cross_ref)


def local_gram(pair_rows):
    rows = pair_rows.shape[0]
    whole = pl.BlockSpec(memory_space=pltpu.VMEM)
    return pl.pallas_call(
        gram_kernel,
        in_specs=[pl.BlockSpec(memory_space=pltpu.HBM)],
        out_specs=whole,
        out_shape=jax.ShapeDtypeStruct((3 * BLOCK, BLOCK), F32),
        scratch_shapes=[
            pltpu.VMEM((WIDTH, WIDTH), F32),
            pltpu.VMEM((WIDTH, WIDTH), F32),
            pltpu.VMEM((rows, WIDTH), F32),
            pltpu.SemaphoreType.DMA((rows // TILE,)),
        ],
        compiler_params=grant(14),
        cost_estimate=pl.CostEstimate(flops=1000, bytes_accessed=1000, transcendentals=0),
        name="gram",
    )(in_hbm(pair_rows))


def cost(rows):
    return pl.CostEstimate(
        flops=6 * rows * WIDTH * WIDTH, bytes_accessed=8 * rows * WIDTH, transcendentals=0
    )


def moved_rows(ends, moved_refs, start, count):
    rows = pl.ds(start, count)
    below, second, above, first = (ref[rows, :] for ref in moved_refs)
    upper = jnp.where(ends[0] == 1, second, below)
    lower = jnp.where(ends[1] == 1, first, above)
    return upper, lower


def moved_tile(ends, moved_refs, row, size):
    return jnp.concatenate(moved_rows(ends, moved_refs, row, size), axis=1)


def moved_gram_kernel(rows, ends, before_ref, *refs):
    moved_refs, (out_ref, total_ref, cross_ref) = refs[:4], refs[4:]
    total_ref[...] = jnp.zeros_like(total_ref)
    cross_ref[...] = jnp.zeros_like(cross_ref)

    def add(row, size, tile):
        add_gram(moved_tile(ends, moved_refs, row, size), total_ref, cross_ref)

    for_tiles(rows, add)

    out_ref[...] = before_ref[...] + pack(total_ref, cross_ref)


def in_vmem(count):
    whole = pl.BlockSpec(memory_space=pltpu.VMEM)
    return [pl.BlockSpec(memory_space=pltpu.SMEM)] + [whole] * count


def moved_gram(ends, before, moved, chunk):
    return pl.pallas_call(
        functools.partial(moved_gram_kernel, chunk),
        in_specs=in_vmem(5),
        out_specs=pl.BlockSpec(memory_space=pltpu.VMEM),
        out_shape=jax.ShapeDtypeStruct((3 * BLOCK, BLOCK), F32),
        scratch_shapes=[pltpu.VMEM((WIDTH, WIDTH), F32)] * 2,
        compiler_params=grant(24),
        cost_estimate=cost(chunk),
        name="moved_gram",
    )(ends, before, *moved)


def row_parts(packed):
    count = lax.axis_size("row")
    step = 1
    while True:
        swap = [(source, source ^ step) for source in range(count)]
        parts = (packed, lax.ppermute(packed, "row", swap))
        step *= 2
        if step >= count:
            return parts
        packed = parts[0] + parts[1]


def outer_product(left, right):
    left1, left2, left3 = three_terms(left)
    right1, right2, right3 = three_terms(right)
    left = jnp.concatenate([left1, left1, left2, left2, left1, left3], axis=0)
    right = jnp.concatenate([right1, right2, right1, right2, right3, right1], axis=0)
    return lax.dot_general(left, right, COLUMNS, preferred_element_type=F32)


def spread(value):
    return jnp.broadcast_to(value, (SUB, BLOCK))


def total(terms):
    while len(terms) > 1:
        paired = [a + b for a, b in zip(terms[::2], terms[1::2])]
        terms = paired + terms[len(terms) - len(terms) % 2 :]
    return terms[0]


def small_inverse(tile, lane, spread_ref, base):
    for j in range(SUB):
        spread_ref[base + SUB * j : base + SUB * (j + 1), :] = spread(tile[:, lane + j : lane + j + 1])
    entry = {
        (i, j): spread_ref[pl.ds(base + SUB * j + i, SUB, stride=0), :]
        for j in range(SUB)
        for i in range(j, SUB)
    }
    lower, scales = {}, []
    for j in range(SUB):
        scale = lax.rsqrt(entry[j, j])
        inverse = scale * scale
        scales.append(scale)
        for i in range(j + 1, SUB):
            lower[i, j] = entry[i, j] * inverse
        for m in range(j + 1, SUB):
            for i in range(m, SUB):
                entry[i, m] = entry[i, m] - lower[i, j] * entry[m, j]
    solved = {}
    for j in range(SUB):
        for i in range(j + 1, SUB):
            terms = [lower[i, j]] + [lower[i, m] * solved[m, j] for m in range(j + 1, i)]
            solved[i, j] = -total(terms)
    solved = {at: value * scales[at[0]] for at, value in solved.items()}
    return solved | {(j, j): scales[j] for j in range(SUB)}


def tiles_of(ref, start, end, first, last):
    return jnp.concatenate([ref[t, start:end, :] for t in range(first, last)], axis=1)


def put_tiles(ref, first, value):
    for t in range(value.shape[1] // BLOCK):
        ref[first + t] = value[:, BLOCK * t : BLOCK * (t + 1)]


def eliminate(work_ref, factor_ref, spread_ref, tiles):
    row = lax.broadcasted_iota(jnp.int32, (SUB, BLOCK), 0)
    lane = lax.broadcasted_iota(jnp.int32, (SUB, BLOCK), 1)
    zero = jnp.zeros((SUB, BLOCK), F32)
    for start in range(0, WIDTH, PANEL):
        end = start + PANEL
        own = start // BLOCK
        for top in range(start, end, SUB):
            at = top % BLOCK
            base = SUB * SUB * (top // SUB % 2)
            small = small_inverse(work_ref[own, top : top + SUB, :], at, spread_ref, base)
            columns = []
            for j in range(SUB):
                column = zero
                for i in range(j, SUB):
                    column = jnp.where(row == i, small[i, j], column)
                columns.append(column)
            for t in range(tiles):
                if t < own:
                    solved = zero
                else:
                    solved = total(
                        [columns[j] * work_ref[t, pl.ds(top + j, SUB, stride=0), :] for j in range(SUB)]
                    )
                    if t == own:
                        solved = jnp.where(lane >= row + at, solved, 0.0)
                factor_ref[t, top : top + SUB, :] = solved
            for below in range(top + SUB, end, SUB):
                tile = work_ref[own, below : below + SUB, :]
                entries = [spread(tile[:, at + j : at + j + 1]) for j in range(SUB)]
                left = [total([entries[j] * small[i, j] for j in range(i + 1)]) for i in range(SUB)]
                for t in range(own, tiles):
                    work_ref[t, below : below + SUB, :] -= total(
                        [left[i] * factor_ref[t, pl.ds(top + i, SUB, stride=0), :] for i in range(SUB)]
                    )
        if end < WIDTH:
            first = end // BLOCK
            update = outer_product(
                tiles_of(factor_ref, start, end, first, WIDTH // BLOCK),
                tiles_of(factor_ref, start, end, first, tiles),
            )
            for t in range(first, tiles):
                here = BLOCK * (t - first)
                work_ref[t, end:, :] -= update[end - BLOCK * first :, here : here + BLOCK]


def rotation_kernel(swap_ref, one_ref, two_ref, first_ref, second_ref, work_ref, factor_ref, spread_ref):
    gram = unpack(one_ref[...] + two_ref[...])
    square = jnp.dot(gram, gram, precision=HIGHEST, preferred_element_type=F32)
    put_tiles(work_ref, 0, square)
    eliminate(work_ref, factor_ref, spread_ref, WIDTH // BLOCK)
    factor = tiles_of(factor_ref, 0, WIDTH, 0, WIDTH // BLOCK)
    square = lax.dot_general(factor, factor, LANES, precision=HIGHEST, preferred_element_type=F32)
    put_tiles(work_ref, 0, square)
    put_tiles(work_ref, WIDTH // BLOCK, factor)
    eliminate(work_ref, factor_ref, spread_ref, 2 * WIDTH // BLOCK)
    halves = [
        tiles_of(factor_ref, start, start + BLOCK, WIDTH // BLOCK, 2 * WIDTH // BLOCK)
        for start in (0, BLOCK)
    ]
    first_ref[...] = jnp.where(swap_ref[0] == 1, halves[1], halves[0])
    second_ref[...] = jnp.where(swap_ref[0] == 1, halves[0], halves[1])


def pair_rotation(swap, parts):
    tiles = pltpu.VMEM((2 * WIDTH // BLOCK, WIDTH, BLOCK), F32)
    return pl.pallas_call(
        rotation_kernel,
        in_specs=[pl.BlockSpec(memory_space=pltpu.SMEM)] + [pl.BlockSpec(memory_space=pltpu.VMEM)] * 2,
        out_shape=[jax.ShapeDtypeStruct((BLOCK, WIDTH), F32)] * 2,
        scratch_shapes=[tiles, tiles, pltpu.VMEM((2 * SUB * SUB, BLOCK), F32)],
        compiler_params=grant(8),
        cost_estimate=pl.CostEstimate(flops=1000, bytes_accessed=1000, transcendentals=0),
        name="rotation",
    )(swap, *parts)


def product(rows, rotation_t):
    high, low = two_terms(rows)
    turn_high, turn_low = two_terms(rotation_t)
    turned = lax.dot_general(high, turn_high, LANES, preferred_element_type=F32)
    turned += lax.dot_general(low, turn_high, LANES, preferred_element_type=F32)
    return turned + lax.dot_general(high, turn_low, LANES, preferred_element_type=F32)


def turn_kernel(start, source_ref, one_ref, two_ref, first_ref, second_ref, rows_ref, sems):
    start_rows(source_ref, rows_ref, sems, start)
    rotation_t = jnp.concatenate([one_ref[...], two_ref[...]])

    def put(row, size, tile):
        row_copy(source_ref, rows_ref, sems, row, size, tile, start).wait()
        rows = pl.ds(row, size)
        turned = product(rows_ref[rows, :], rotation_t)
        first_ref[rows, :] = turned[:, :BLOCK]
        second_ref[rows, :] = turned[:, BLOCK:]

    for_tiles(rows_ref.shape[0], put)


def turn(pair_rows, rotation_t, start, rows):
    whole = pl.BlockSpec(memory_space=pltpu.VMEM)
    return pl.pallas_call(
        functools.partial(turn_kernel, start),
        in_specs=[pl.BlockSpec(memory_space=pltpu.HBM), whole, whole],
        out_specs=[whole, whole],
        out_shape=[jax.ShapeDtypeStruct((rows, BLOCK), F32)] * 2,
        scratch_shapes=[
            pltpu.VMEM((rows, WIDTH), F32),
            pltpu.SemaphoreType.DMA((pl.cdiv(rows, TILE),)),
        ],
        compiler_params=grant(24),
        cost_estimate=cost(rows),
        name="turn",
    )(in_hbm(pair_rows), *rotation_t)


def last_turn_kernel(ends, one_ref, two_ref, *refs):
    arrays = 4 * len(CHUNKS)
    moved = [refs[at : at + 4] for at in range(0, arrays, 4)]
    out_ref, turned_ref, sems = refs[arrays:]
    rotation_t = jnp.concatenate([one_ref[...], two_ref[...]])

    def out_copy(row, size, sem):
        rows = pl.ds(pl.multiple_of(row, BLOCK), size)
        return pltpu.make_async_copy(turned_ref.at[rows, :], out_ref.at[rows, :], sems.at[sem])

    start, sem = 0, 0
    copies = []
    for moved_refs, count in zip(moved, CHUNKS):

        def put(row, size, tile, moved_refs=moved_refs, start=start, sem=sem):
            rows = moved_tile(ends, moved_refs, row, size)
            at = pl.ds(pl.multiple_of(start + row, BLOCK), size)
            turned_ref[at, :] = product(rows, rotation_t)
            out_copy(start + row, size, sem + tile).start()

        for_tiles(count, put)
        for row in range(0, count, TILE):
            copies.append((start + row, min(TILE, count - row), sem))
            sem += 1
        start += count
    for copy in copies:
        out_copy(*copy).wait()


def last_turn(ends, rotation_t, moved):
    rows = sum(CHUNKS)
    tiles = sum(pl.cdiv(count, TILE) for count in CHUNKS)
    moved = [array for part in moved for array in part]
    return pl.pallas_call(
        last_turn_kernel,
        in_specs=in_vmem(2 + len(moved)),
        out_specs=pl.BlockSpec(memory_space=pl.ANY),
        out_shape=jax.ShapeDtypeStruct((rows, WIDTH), F32),
        scratch_shapes=[
            pltpu.VMEM((rows, WIDTH), F32),
            pltpu.SemaphoreType.DMA((tiles,)),
        ],
        compiler_params=grant(24),
        cost_estimate=cost(rows),
        name="last_turn",
    )(ends, *rotation_t, *moved)


def send_up(value):
    count = lax.axis_size("col")
    return lax.ppermute(value, "col", [(p, p + 1) for p in range(count - 1)])


def send_down(value):
    count = lax.axis_size("col")
    return lax.ppermute(value, "col", [(p, p - 1) for p in range(1, count)])


def local(diffs, pairing):
    col_count = lax.axis_size("col")
    position = lax.axis_index("col")
    local_rows = diffs.shape[0]
    rows = col_count * local_rows
    bottom, top = position == 0, position == col_count - 1
    ends = jnp.stack([bottom, top]).astype(jnp.int32)
    ordered = order_pairs(diffs, pairing)
    pair_rows = lax.all_to_all(ordered, "col", split_axis=0, concat_axis=0, tiled=True)
    pair_rows = pair_rows.reshape(rows, WIDTH)

    rotation_t = pair_rotation(ends[:1], row_parts(local_gram(pair_rows)))
    moved, start = [], 0
    for chunk in CHUNKS:
        first, second = turn(pair_rows, rotation_t, start, chunk)
        moved.append((send_up(first), second, send_down(second), first))
        start += chunk
    gram = jnp.zeros((3 * BLOCK, BLOCK), F32)
    for part, chunk in zip(moved, CHUNKS):
        gram = moved_gram(ends, gram, part, chunk)
    rotation_t = pair_rotation(jnp.zeros((1,), jnp.int32), row_parts(gram))
    return last_turn(ends, rotation_t, moved).reshape(col_count, 1, local_rows, WIDTH)


def solution(mesh):
    in_specs = (P(("col", "row"), None), P())
    out_specs = P(None, "row", None, "col")
    return jax.shard_map(local, mesh=mesh, in_specs=in_specs, out_specs=out_specs, check_vma=False)
```
